32 devices in a mesh: node: 8 (over z, y), local: 4 (over x, core).
Axes of the slice: x: 2, y: 2, z: 4, core: 2. Of those that a mesh axis runs over, the one named last changes fastest.
Arguments:
- inputs: bfloat16 [64, 3584], P('node', 'local'), may hold values from -6 to 6
- out_grad: bfloat16 [64, 3584], P('node', 'local'), may hold values from -6 to 6
- expert_ids: int32 [64, 2], replicated, may hold values from 0 to 7, all different within a row; in each aligned block of 64 rows (0 to 63, 64 to 127, ...) at most 32 rows name the same one
- route_probs: float32 [64, 2], replicated, may hold values from 0.1 to 1
- gate_weight: bfloat16 [8, 3584, 1024], P('node', None, 'local'), may hold values from -0.09375 to 0.09375
- up_weight: bfloat16 [8, 3584, 1024], P('node', None, 'local'), may hold values from -0.09375 to 0.09375
- down_weight: bfloat16 [8, 1024, 3584], P('node', 'local'), may hold values from -0.1875 to 0.1875
Outputs:
- d_inputs: bfloat16 [64, 3584], P('node', 'local')
The draws below stay inside these ranges and needn't reach their ends.
Inputs may be any that keep to these rules, and one draw needn't show every extreme that they name: `expert_ids`: each row names 2 different experts. No expert is named by more than 32 pairs in all, a bound that some block reaches.
All inputs are finite; a program needn't handle non-finite values.
Results may differ from the reference program's by a relative error of at most 0.0064.
Values may be sent and summed in bfloat16 or wider, within the bound.
No kernel may reach another device: no remote copies, remote signals or barrier semaphores. Data moves between devices by JAX's collectives and lax.ppermute only.
A program may use at most 64 MiB of HBM per device.

```python
import math
import jax
import jax.numpy as jnp
import numpy as np
from jax import lax

D = 3584
FF = 1024
TOP = 2
CAPE = 32
TOKENS = 64
EXPERTS = 8


def block_scale(rng, dims, split, least, top_value):
    def one(dim, blocks):
        draws = jax.random.uniform(jax.random.fold_in(jax.random.fold_in(rng, 6), dim), (blocks,), jnp.float32, least / len(split), top_value / len(split))
        return jnp.repeat(jnp.exp(draws), dims[dim] // blocks).reshape((-1,) + (1,) * (len(dims) - dim - 1))

    factor_of = one(*split[0])
    for cut in split[1:]:
        factor_of = factor_of * one(*cut)
    return factor_of


def deal_out(key, own, number, rows, count, top, bound, lean):
    sequence = jax.random.permutation(key, count)
    crowded, usual = load_shares(count, rows * top, bound, lean, True), load_shares(count, rows * top, bound, lean, False)
    places = jnp.arange(count)

    def named(sizes, rotation):
        used = int((sizes > 0).sum())
        fixed = max(1, used // 4)
        passed = fixed + (places - fixed + rotation * (used - fixed)) % max(1, count - fixed)
        return jnp.zeros((count,), jnp.int32).at[sequence[jnp.where(places < fixed, places, passed)]].set(jnp.asarray(sizes, jnp.int32))

    sizes = jnp.where(number % 4 == 0, named(crowded, number // 4), named(usual, number - number // 4 - 1))
    mixed = jax.random.permutation(jax.random.fold_in(own, 3), count)
    donor, taker = mixed[0:count // 2 * 2:2], mixed[1:count // 2 * 2:2]
    room = jnp.minimum(sizes[donor] - 1, bound - sizes[taker]) // 2
    room = jnp.where((donor == sequence[0]) | (taker == sequence[0]) | (sizes[taker] == 0), 0, jnp.maximum(room, 0))
    passed = jax.random.randint(jax.random.fold_in(own, 4), (count // 2,), 0, 1 << 20) % (room + 1)
    sizes = sizes.at[donor].add(-passed).at[taker].add(passed)
    members = jnp.searchsorted(jnp.cumsum(sizes), jnp.arange(rows * top), side="right").astype(jnp.int32)
    grid = members.reshape(top, rows).T
    grid = grid[jax.random.permutation(jax.random.fold_in(own, 1), rows)]
    rotation = jax.random.randint(jax.random.fold_in(own, 2), (rows, 1), 0, top)
    return jnp.take_along_axis(grid, (jnp.arange(top)[None, :] + rotation) % top, axis=1)


def load_shares(amount, total, reach, lean, full):
    weights = [(1 << 20) // math.isqrt(standing ** lean) + 1 for standing in range(1, amount + 1)]
    largest = reach if full else min(reach, max(-(-total // amount), total * weights[0] // sum(weights)))
    least = 1 if total - largest >= amount - 1 else 0
    given, surplus = [largest] + [least] * (amount - 1), total - largest - least * (amount - 1)
    while surplus > 0:
        candidates = [i for i in range(1, amount) if given[i] < largest] or [i for i in range(1, amount) if given[i] < reach]
        mass, budget = sum([weights[i] for i in candidates]), surplus
        for i in candidates:
            extra = min(reach - given[i], max(1, budget * weights[i] // mass), surplus)
            given[i] = given[i] + extra
            surplus = surplus - extra
    return np.array(given)


def bell_draw(rng, dims, spread, most, shards=(), kind=jnp.bfloat16):
    result = spread * jax.random.normal(rng, dims, jnp.float32)
    if shards:
        result = result * block_scale(rng, dims, shards, -0.22, 0.18)
    return jnp.clip(result, -most, most).astype(kind)


def setup_inputs(seed: int = 0) -> dict:
    streams_of = jax.random.split(jax.random.key(seed), 8)
    inputs = bell_draw(streams_of[0], (TOKENS, D), 1.0, 6.0, ((0, 8), (1, 4)))
    out_grad = bell_draw(streams_of[1], (TOKENS, D), 1.0, 6.0, ((0, 8), (1, 4)))
    expert_ids_keys = jax.random.split(jax.random.fold_in(streams_of[2], 1), TOKENS // TOKENS)
    expert_ids_turns = jax.random.permutation(jax.random.fold_in(streams_of[2], 3), TOKENS // TOKENS)
    expert_ids = jax.vmap(lambda own, number: deal_out(jax.random.fold_in(streams_of[2], 2), own, number, TOKENS, EXPERTS, TOP, CAPE, 2))(expert_ids_keys, expert_ids_turns).reshape((TOKENS, TOP))
    route_probs = jnp.clip(jax.random.uniform(streams_of[3], (TOKENS, TOP), jnp.float32, 0.1, 1.0), 0.1, 1.0)
    gate_weight = bell_draw(streams_of[4], (EXPERTS, D, FF), D ** -0.5, 0.09375, ((0, 8), (2, 4)))
    up_weight = bell_draw(streams_of[5], (EXPERTS, D, FF), D ** -0.5, 0.09375, ((0, 8), (2, 4)))
    down_weight = bell_draw(streams_of[6], (EXPERTS, FF, D), FF ** -0.5, 0.1875, ((0, 8), (1, 4)))
    return dict(inputs=inputs, out_grad=out_grad, expert_ids=expert_ids, route_probs=route_probs, gate_weight=gate_weight, up_weight=up_weight, down_weight=down_weight)


def slot_tables(expert_ids, route_probs, expert, cape):
    flat = expert_ids.reshape(-1)
    hit = (flat == expert).astype(jnp.int32)
    rank = jnp.cumsum(hit).astype(jnp.int32) - 1
    slots = jnp.arange(cape, dtype=jnp.int32)
    onehot = jnp.where((rank[None, :] == slots[:, None]) & (hit[None, :] == 1), 1.0, 0.0).astype(jnp.float32)
    onehot = onehot.reshape(cape, expert_ids.shape[0], expert_ids.shape[1])
    select = jnp.sum(onehot, axis=2)
    scale = jnp.sum(onehot * route_probs[None, :, :], axis=(1, 2))
    return select, scale


def expert_terms(x_rows, g_rows, gate_w, up_w, down_w):
    gate = jnp.dot(x_rows, gate_w, preferred_element_type=jnp.float32)
    up = jnp.dot(x_rows, up_w, preferred_element_type=jnp.float32)
    sig = jax.nn.sigmoid(gate)
    act = gate * sig
    d_hidden = lax.dot_general(g_rows, down_w, (((1,), (1,)), ((), ())), preferred_element_type=jnp.float32)
    d_up = (d_hidden * act).astype(jnp.bfloat16)
    d_gate = (d_hidden * up * sig * (1.0 + gate * (1.0 - sig))).astype(jnp.bfloat16)
    first = lax.dot_general(d_gate, gate_w, (((1,), (1,)), ((), ())), preferred_element_type=jnp.float32)
    second = lax.dot_general(d_up, up_w, (((1,), (1,)), ((), ())), preferred_element_type=jnp.float32)
    return first + second


def reference(inputs, out_grad, expert_ids, route_probs, gate_weight, up_weight, down_weight):
    def one_expert(carry, expert):
        select, scale = slot_tables(expert_ids, route_probs, expert, CAPE)
        sel_half = select.astype(jnp.bfloat16)
        x_rows = jnp.dot(sel_half, inputs, preferred_element_type=jnp.float32).astype(jnp.bfloat16)
        g_sum = jnp.dot(sel_half, out_grad, preferred_element_type=jnp.float32)
        g_rows = (scale[:, None] * g_sum).astype(jnp.bfloat16)
        d_rows = expert_terms(x_rows, g_rows, gate_weight[expert], up_weight[expert], down_weight[expert]).astype(jnp.bfloat16)
        back = lax.dot_general(sel_half, d_rows, (((0,), (0,)), ((), ())), preferred_element_type=jnp.float32)
        return carry + back, None

    total, _ = lax.scan(one_expert, jnp.zeros((TOKENS, D), jnp.float32), jnp.arange(EXPERTS, dtype=jnp.int32))
    return total.astype(jnp.bfloat16)
```

```python
import jax
import jax.numpy as jnp
from jax import lax
from jax.sharding import PartitionSpec as P


def slot_tables(expert_ids, route_probs, expert, cape):
    hit = expert_ids == expert
    tokens = expert_ids.shape[0]
    once = jnp.sum(hit.astype(jnp.float32), axis=1)
    scale = jnp.sum(jnp.where(hit, route_probs, 0.0), axis=1)
    row = lax.broadcasted_iota(jnp.int32, (tokens, tokens), 0)
    col = lax.broadcasted_iota(jnp.int32, (tokens, tokens), 1)
    rank = jnp.sum(jnp.where(col < row, once[None, :], 0.0), axis=1)
    slots = lax.broadcasted_iota(jnp.int32, (cape, tokens), 0).astype(jnp.float32)
    select = jnp.where((rank[None, :] == slots) & (once[None, :] > 0.5), 1.0, 0.0)
    return select, jnp.sum(select * scale[None, :], axis=1)


def partners(size, step):
    if size & (size - 1) == 0:
        return [(i, i ^ step) for i in range(size)]
    return [(i, (i + step) % size) for i in range(size)]


def source(size, me, step):
    if size & (size - 1) == 0:
        return me ^ step
    return lax.rem(me + (size - step), size)


def target(size, me, step):
    if size & (size - 1) == 0:
        return me ^ step
    return lax.rem(me + step, size)


def shards(nodes, locals_, inputs, out_grad, expert_ids, route_probs, gate_w, up_w, down_w):
    expert = lax.axis_index("node")
    me = lax.axis_index("local")
    rows, width = inputs.shape
    cape = 2 * rows * expert_ids.shape[1]
    select, scale = slot_tables(expert_ids, route_probs, expert, cape)
    sel = select.astype(jnp.bfloat16)

    block = jnp.stack([inputs, out_grad])
    every = lax.all_to_all(
        jnp.broadcast_to(block[None], (nodes,) + block.shape), "node", 0, 0, tiled=True
    )
    every_x = every[:, 0].reshape(nodes * rows, width)
    every_g = every[:, 1].reshape(nodes * rows, width)
    x_part = jnp.dot(sel, every_x, preferred_element_type=jnp.float32).astype(jnp.bfloat16)
    g_sum = jnp.dot(sel, every_g, preferred_element_type=jnp.float32)
    g_part = (scale[:, None] * g_sum).astype(jnp.bfloat16)
    part = jnp.concatenate([x_part, g_part], axis=0)

    whole = jnp.zeros((2 * cape, width * locals_), jnp.bfloat16)
    whole = lax.dynamic_update_slice(whole, part, (0, me * width))
    for step in range(1, locals_):
        got = lax.ppermute(part, "local", partners(locals_, step))
        whole = lax.dynamic_update_slice(whole, got, (0, source(locals_, me, step) * width))
    x_rows, g_rows = whole[:cape], whole[cape:]

    gate = jnp.dot(x_rows, gate_w[0], preferred_element_type=jnp.float32)
    up = jnp.dot(x_rows, up_w[0], preferred_element_type=jnp.float32)
    sig = jax.nn.sigmoid(gate)
    d_hidden = lax.dot_general(
        g_rows, down_w[0], (((1,), (1,)), ((), ())), preferred_element_type=jnp.float32
    )
    d_up = (d_hidden * (gate * sig)).astype(jnp.bfloat16)
    d_gate = (d_hidden * up * sig * (1.0 + gate * (1.0 - sig))).astype(jnp.bfloat16)
    partial = lax.dot_general(
        d_gate, gate_w[0], (((1,), (1,)), ((), ())), preferred_element_type=jnp.float32
    ) + lax.dot_general(
        d_up, up_w[0], (((1,), (1,)), ((), ())), preferred_element_type=jnp.float32
    )

    half = partial.astype(jnp.bfloat16)
    total = lax.dynamic_slice_in_dim(partial, me * width, width, 1)
    for step in range(1, locals_):
        piece = lax.dynamic_slice_in_dim(half, target(locals_, me, step) * width, width, 1)
        total = total + lax.ppermute(piece, "local", partners(locals_, step)).astype(jnp.float32)
    d_rows = total.astype(jnp.bfloat16)

    back = lax.dot_general(
        sel, d_rows, (((0,), (0,)), ((), ())), preferred_element_type=jnp.float32
    ).astype(jnp.bfloat16)
    mine = lax.all_to_all(back.reshape(nodes, rows, width), "node", 0, 0, tiled=True)
    return jnp.sum(mine.astype(jnp.float32), axis=0).astype(jnp.bfloat16)


def solution(mesh):
    placed = (
        P("node", "local"),
        P("node", "local"),
        P(),
        P(),
        P("node", None, "local"),
        P("node", None, "local"),
        P("node", "local", None),
    )

    def body(*args):
        return shards(mesh.shape["node"], mesh.shape["local"], *args)

    return jax.shard_map(
        body, mesh=mesh, in_specs=placed, out_specs=P("node", "local"), check_vma=False
    )
```

```python
import functools

import jax
import jax.numpy as jnp
from jax import lax
from jax.experimental import pallas as pl
from jax.experimental.pallas import tpu as pltpu
from jax.sharding import PartitionSpec as P

F32 = jnp.float32
BF16 = jnp.bfloat16
NT = (((1,), (1,)), ((), ()))


def slot_tables(expert_ids, route_probs, expert, cape):
    hit = expert_ids == expert
    tokens = expert_ids.shape[0]
    once = jnp.sum(hit.astype(F32), axis=1)
    scale = jnp.sum(jnp.where(hit, route_probs, 0.0), axis=1)
    row = lax.broadcasted_iota(jnp.int32, (tokens, tokens), 0)
    col = lax.broadcasted_iota(jnp.int32, (tokens, tokens), 1)
    rank = jnp.sum(jnp.where(col < row, once[None, :], 0.0), axis=1)
    slots = lax.broadcasted_iota(jnp.int32, (cape, tokens), 0).astype(F32)
    select = jnp.where((rank[None, :] == slots) & (once[None, :] > 0.5), 1.0, 0.0)
    return select, jnp.sum(select * scale[None, :], axis=1)


def partners(size, step):
    if size & (size - 1) == 0:
        return [(i, i ^ step) for i in range(size)]
    return [(i, (i + step) % size) for i in range(size)]


def source(size, me, step):
    if size & (size - 1) == 0:
        return me ^ step
    return lax.rem(me + (size - step), size)


def target(size, me, step):
    if size & (size - 1) == 0:
        return me ^ step
    return lax.rem(me + step, size)


def hidden_terms(gate, up, d_hidden):
    sig = jax.nn.sigmoid(gate)
    d_up = (d_hidden * (gate * sig)).astype(BF16)
    d_gate = (d_hidden * up * sig * (1.0 + gate * (1.0 - sig))).astype(BF16)
    return d_gate, d_up


def general(nodes, locals_, inputs, out_grad, expert_ids, route_probs, gate_w, up_w, down_w):
    expert = lax.axis_index("node")
    me = lax.axis_index("local")
    rows, width = inputs.shape
    cape = 2 * rows * expert_ids.shape[1]
    select, scale = slot_tables(expert_ids, route_probs, expert, cape)
    sel = select.astype(BF16)

    block = jnp.concatenate([inputs, out_grad], axis=0)
    every = lax.all_to_all(
        jnp.broadcast_to(block[None], (nodes,) + block.shape), "node", 0, 0, tiled=True
    )
    s3 = sel.reshape(cape, nodes, 1, rows)
    none = jnp.zeros_like(s3)
    pick = jnp.concatenate(
        [
            jnp.concatenate([s3, none], axis=2).reshape(cape, nodes * 2 * rows),
            jnp.concatenate([none, s3], axis=2).reshape(cape, nodes * 2 * rows),
        ],
        axis=0,
    )
    factor = jnp.concatenate([jnp.ones_like(scale), scale])
    part = jnp.dot(pick, every.reshape(nodes * 2 * rows, width), preferred_element_type=F32)
    part = (factor[:, None] * part).astype(BF16)

    pieces = [part] + [
        lax.ppermute(part, "local", partners(locals_, step)) for step in range(1, locals_)
    ]
    whole = jnp.zeros((2 * cape, width * locals_), BF16)
    for step in range(locals_):
        whole = lax.dynamic_update_slice(
            whole, pieces[step], (0, source(locals_, me, step) * width)
        )
    gate = jnp.dot(whole[:cape], gate_w[0], preferred_element_type=F32)
    up = jnp.dot(whole[:cape], up_w[0], preferred_element_type=F32)
    d_hidden = lax.dot_general(whole[cape:], down_w[0], NT, preferred_element_type=F32)
    d_gate, d_up = hidden_terms(gate, up, d_hidden)
    partial = lax.dot_general(
        d_gate, gate_w[0], NT, preferred_element_type=F32
    ) + lax.dot_general(d_up, up_w[0], NT, preferred_element_type=F32)
    half = partial.astype(BF16)
    total = lax.dynamic_slice_in_dim(partial, me * width, width, 1)
    sent = [
        lax.dynamic_slice_in_dim(half, target(locals_, me, step) * width, width, 1)
        for step in range(1, locals_)
    ]
    for step in range(1, locals_):
        total = total + lax.ppermute(sent[step - 1], "local", partners(locals_, step)).astype(F32)
    d_rows = total.astype(BF16)

    back = lax.dot_general(
        sel, d_rows, (((0,), (0,)), ((), ())), preferred_element_type=F32
    ).astype(BF16)
    mine = lax.all_to_all(back.reshape(nodes, rows, width), "node", 0, 0, tiled=True)
    return jnp.sum(mine.astype(F32), axis=0).astype(BF16)


def column(width, index):
    return pl.ds(pl.multiple_of(index * width, width), width)


def place():
    return 2 * lax.axis_index("outer") + lax.axis_index("inner")


def block_terms(piece, cape, at, gate_ref, up_ref, down_ref):
    x, g = piece[:cape, :], piece[cape:, :]
    return (
        jnp.dot(x, gate_ref[at, :], preferred_element_type=F32),
        jnp.dot(x, up_ref[at, :], preferred_element_type=F32),
        lax.dot_general(g, down_ref[:, at], NT, preferred_element_type=F32),
    )


def first_kernel(cape, own, near, gate_hbm, up_hbm, down_hbm, acc, gate_ref, up_ref, down_ref, sems):
    me = place()
    width = own.shape[1]
    order = [me, me ^ 1, me ^ 2, me ^ 3]
    copies = []
    for step, block in enumerate(order):
        at = column(width, block)
        copies.append(
            [
                pltpu.make_async_copy(gate_hbm.at[at, :], gate_ref.at[at, :], sems.at[0, step]),
                pltpu.make_async_copy(up_hbm.at[at, :], up_ref.at[at, :], sems.at[1, step]),
                pltpu.make_async_copy(down_hbm.at[:, at], down_ref.at[:, at], sems.at[2, step]),
            ]
        )
    for group in copies:
        for copy in group:
            copy.start()
    sums = None
    for step, piece in enumerate((own, near)):
        for copy in copies[step]:
            copy.wait()
        terms = block_terms(piece, cape, column(width, order[step]), gate_ref, up_ref, down_ref)
        sums = terms if sums is None else [a + b for a, b in zip(sums, terms)]
    for index in range(3):
        acc[index] = sums[index]
    for group in copies[2:]:
        for copy in group:
            copy.wait()


def third_kernel(cape, piece, acc, gate_ref, up_ref, down_ref, out):
    at = column(piece.shape[1], place() ^ 2)
    for index, term in enumerate(block_terms(piece, cape, at, gate_ref, up_ref, down_ref)):
        out[index] = acc[index] + term


def down_terms(d_gate, d_up, at, gate_ref, up_ref):
    return lax.dot_general(
        d_gate, gate_ref[at, :], NT, preferred_element_type=F32
    ) + lax.dot_general(d_up, up_ref[at, :], NT, preferred_element_type=F32)


def hidden_kernel(cape, piece, acc, gate_ref, up_ref, down_ref, sent, d_gate_ref, d_up_ref):
    me = place()
    width = piece.shape[1]
    terms = block_terms(piece, cape, column(width, me ^ 3), gate_ref, up_ref, down_ref)
    gate, up, d_hidden = [acc[index] + term for index, term in enumerate(terms)]
    d_gate, d_up = hidden_terms(gate, up, d_hidden)
    d_gate_ref[...] = d_gate
    d_up_ref[...] = d_up
    inner = (me & 1) ^ 1
    for outer in range(2):
        at = column(width, 2 * outer + inner)
        sent[:, outer * width : (outer + 1) * width] = down_terms(
            d_gate, d_up, at, gate_ref, up_ref
        ).astype(BF16)


def own_kernel(d_gate_ref, d_up_ref, gate_ref, up_ref, own):
    width = own.shape[1] // 2
    inner = place() & 1
    for outer in range(2):
        at = column(width, 2 * outer + inner)
        own[:, outer * width : (outer + 1) * width] = down_terms(
            d_gate_ref[...], d_up_ref[...], at, gate_ref, up_ref
        )


def call(name, body, outs, *args, hbm=(), scratch=(), limit=4, nbytes=1 << 18):
    args = [
        pltpu.with_memory_space_constraint(arg, pltpu.HBM) if index in hbm else arg
        for index, arg in enumerate(args)
    ]
    vmem = pl.BlockSpec(memory_space=pltpu.VMEM)
    far = pl.BlockSpec(memory_space=pltpu.HBM)
    return pl.pallas_call(
        body,
        out_shape=[jax.ShapeDtypeStruct(shape, dtype) for shape, dtype in outs],
        in_specs=[far if index in hbm else vmem for index in range(len(args))],
        out_specs=[vmem] * len(outs),
        scratch_shapes=list(scratch),
        compiler_params=pltpu.CompilerParams(vmem_limit_bytes=limit << 20),
        cost_estimate=pl.CostEstimate(flops=0, transcendentals=0, bytes_accessed=nbytes),
        name=name,
    )(*args)


def spread_kernel(
    cape, x_hbm, g_hbm, ids_hbm, probs_hbm, out, pick, factor, sel, x_ref, g_ref, ids_ref, probs_ref, sems
):
    pairs = ((ids_hbm, ids_ref), (probs_hbm, probs_ref), (x_hbm, x_ref), (g_hbm, g_ref))
    copies = [
        pltpu.make_async_copy(source_ref, there, sems.at[index])
        for index, (source_ref, there) in enumerate(pairs)
    ]
    for copy in copies:
        copy.start()
    nodes, block, _ = out.shape
    rows = block // 2
    tokens = ids_ref.shape[1]
    shift = block.bit_length() - 1

    def grid(height, width, axis):
        return lax.broadcasted_iota(jnp.int32, (height, width), axis)

    before = (grid(tokens, tokens, 0) < grid(tokens, tokens, 1)).astype(BF16)
    token = grid(tokens, nodes * block, 0)
    lane = grid(tokens, nodes * block, 1)
    spread = (token == (lane >> shift) * rows + (lane & (rows - 1))).astype(BF16)
    slot = grid(2 * cape, nodes * block, 0)
    side = (grid(2 * cape, nodes * block, 1) & (block - 1)) >= rows

    copies[0].wait()
    hit = ids_ref[...] == lax.axis_index("node")
    once = jnp.sum(jnp.where(hit, 1.0, 0.0), axis=0, keepdims=True)
    wide = jnp.broadcast_to(once, (8, tokens)).astype(BF16)
    rank = jnp.dot(wide, before, preferred_element_type=F32)
    code = jnp.where(wide > 0.5, rank, -2.0 * cape)
    mine = code[:1, :] == grid(cape, tokens, 0).astype(F32)
    sel[...] = jnp.where(mine, 1.0, 0.0).astype(BF16)
    there = jnp.dot(code.astype(BF16), spread, preferred_element_type=F32)[:1, :]
    target_slot = jnp.where(side, slot - cape, slot).astype(F32)
    pick[...] = jnp.where(there == target_slot, 1.0, 0.0).astype(BF16)
    copies[1].wait()
    scale = jnp.sum(jnp.where(hit, probs_ref[...], 0.0), axis=0, keepdims=True)
    factor[:cape, :] = jnp.ones((cape, 1), F32)
    factor[cape:, :] = jnp.sum(jnp.where(mine, scale, 0.0), axis=1, keepdims=True)
    copies[2].wait()
    copies[3].wait()
    for node in range(nodes):
        out[node, :rows, :] = x_ref[...]
        out[node, rows:, :] = g_ref[...]


def pick_kernel(pick, factor, every, own):
    part = jnp.dot(pick[...], every[...], preferred_element_type=F32)
    own[...] = (factor[...] * part).astype(BF16)


def shards(nodes, inputs, out_grad, expert_ids, route_probs, gate_w, up_w, down_w):
    gate_w, up_w, down_w = gate_w[0], up_w[0], down_w[0]
    rows, width = inputs.shape
    cape = 2 * rows * expert_ids.shape[1]
    swap = [(0, 1), (1, 0)]

    tokens = nodes * rows
    block, pick, factor, sel = call(
        "spread",
        functools.partial(spread_kernel, cape),
        [
            ((nodes, 2 * rows, width), BF16),
            ((2 * cape, 2 * tokens), BF16),
            ((2 * cape, 1), F32),
            ((cape, tokens), BF16),
        ],
        inputs, out_grad, expert_ids.T, route_probs.T,
        hbm=(0, 1, 2, 3),
        scratch=[
            pltpu.VMEM((rows, width), BF16),
            pltpu.VMEM((rows, width), BF16),
            pltpu.VMEM(expert_ids.shape[::-1], jnp.int32),
            pltpu.VMEM(route_probs.shape[::-1], F32),
            pltpu.SemaphoreType.DMA((4,)),
        ],
    )
    every = lax.all_to_all(block, "node", 0, 0, tiled=True)
    (own,) = call(
        "pick",
        pick_kernel,
        [((2 * cape, width), BF16)],
        pick, factor, every.reshape(2 * tokens, width),
    )
    far = lax.ppermute(own, "outer", swap)
    near = lax.ppermute(own, "inner", swap)
    hidden = down_w.shape[0]
    acc, gate_v, up_v, down_v = call(
        "first",
        functools.partial(first_kernel, cape),
        [((3, cape, hidden), F32)] + [(w.shape, BF16) for w in (gate_w, up_w, down_w)],
        own, near, gate_w, up_w, down_w,
        hbm=(2, 3, 4),
        scratch=[pltpu.SemaphoreType.DMA((3, 4))],
        nbytes=6 << 20,
    )
    far, acc = lax.optimization_barrier((far, acc))
    across = lax.ppermute(far, "inner", swap)
    (acc,) = call(
        "third",
        functools.partial(third_kernel, cape),
        [((3, cape, hidden), F32)],
        far, acc, gate_v, up_v, down_v,
    )
    sent, d_gate, d_up = call(
        "hidden",
        functools.partial(hidden_kernel, cape),
        [((cape, 2 * width), BF16), ((cape, hidden), BF16), ((cape, hidden), BF16)],
        across, acc, gate_v, up_v, down_v,
    )
    got = lax.ppermute(sent, "inner", swap)
    (mine,) = call("own", own_kernel, [((cape, 2 * width), F32)], d_gate, d_up, gate_v, up_v)
    half = (mine + got.astype(F32)).astype(BF16)
    back = lax.dot_general(
        sel, half, (((0,), (0,)), ((), ())), preferred_element_type=F32
    ).astype(BF16)
    back = back.reshape(nodes, rows, 2, width).transpose(0, 2, 1, 3)
    home = lax.all_to_all(
        back.reshape(2 * nodes, rows, width), ("node", "outer"), 0, 0, tiled=True
    )
    return jnp.sum(home.astype(F32), axis=0).astype(BF16)


def solution(mesh):
    nodes, locals_ = mesh.shape["node"], mesh.shape["local"]

    def program(inputs, *args):
        width = inputs.shape[1] // locals_
        rows = inputs.shape[0] // nodes
        if locals_ == 4 and width % 128 == 0 and rows & (rows - 1) == 0:
            fine = jax.sharding.Mesh(
                mesh.devices.reshape(nodes, locals_ // 2, 2), ("node", "outer", "inner")
            )
            local = ("outer", "inner")
            body = functools.partial(shards, nodes)
        else:
            fine, local = mesh, "local"
            body = functools.partial(general, nodes, locals_)
        placed = (
            P("node", local),
            P("node", local),
            P(),
            P(),
            P("node", None, local),
            P("node", None, local),
            P("node", local, None),
        )
        return jax.shard_map(
            body, mesh=fine, in_specs=placed, out_specs=P("node", local), check_vma=False
        )(inputs, *args)

    return program
```

```python
import functools

import jax
import jax.numpy as jnp
from jax import lax
from jax.experimental import pallas as pl
from jax.experimental.pallas import tpu as pltpu
from jax.sharding import PartitionSpec as P


F32 = jnp.float32
BF16 = jnp.bfloat16
NT = (((1,), (1,)), ((), ()))


def slot_tables(expert_ids, route_probs, expert, cape):
    hit = expert_ids == expert
    tokens = expert_ids.shape[0]
    once = jnp.sum(hit.astype(F32), axis=1)
    scale = jnp.sum(jnp.where(hit, route_probs, 0.0), axis=1)
    row = lax.broadcasted_iota(jnp.int32, (tokens, tokens), 0)
    col = lax.broadcasted_iota(jnp.int32, (tokens, tokens), 1)
    rank = jnp.sum(jnp.where(col < row, once[None, :], 0.0), axis=1)
    slots = lax.broadcasted_iota(jnp.int32, (cape, tokens), 0).astype(F32)
    select = jnp.where((rank[None, :] == slots) & (once[None, :] > 0.5), 1.0, 0.0)
    return select, jnp.sum(select * scale[None, :], axis=1)


def partners(size, step):
    if size & (size - 1) == 0:
        return [(i, i ^ step) for i in range(size)]
    return [(i, (i + step) % size) for i in range(size)]


def source(size, me, step):
    if size & (size - 1) == 0:
        return me ^ step
    return lax.rem(me + (size - step), size)


def target(size, me, step):
    if size & (size - 1) == 0:
        return me ^ step
    return lax.rem(me + step, size)


def hidden_terms(gate, up, d_hidden):
    sig = jax.nn.sigmoid(gate)
    d_up = (d_hidden * (gate * sig)).astype(BF16)
    d_gate = (d_hidden * up * sig * (1.0 + gate * (1.0 - sig))).astype(BF16)
    return d_gate, d_up


def general(nodes, locals_, inputs, out_grad, expert_ids, route_probs, gate_w, up_w, down_w):
    expert = lax.axis_index("node")
    me = lax.axis_index("local")
    rows, width = inputs.shape
    cape = 2 * rows * expert_ids.shape[1]
    select, scale = slot_tables(expert_ids, route_probs, expert, cape)
    sel = select.astype(BF16)

    block = jnp.concatenate([inputs, out_grad], axis=0)
    every = lax.all_to_all(
        jnp.broadcast_to(block[None], (nodes,) + block.shape), "node", 0, 0, tiled=True
    )
    s3 = sel.reshape(cape, nodes, 1, rows)
    none = jnp.zeros_like(s3)
    pick = jnp.concatenate(
        [
            jnp.concatenate([s3, none], axis=2).reshape(cape, nodes * 2 * rows),
            jnp.concatenate([none, s3], axis=2).reshape(cape, nodes * 2 * rows),
        ],
        axis=0,
    )
    factor = jnp.concatenate([jnp.ones_like(scale), scale])
    part = jnp.dot(pick, every.reshape(nodes * 2 * rows, width), preferred_element_type=F32)
    part = (factor[:, None] * part).astype(BF16)

    pieces = [part] + [
        lax.ppermute(part, "local", partners(locals_, step)) for step in range(1, locals_)
    ]
    whole = jnp.zeros((2 * cape, width * locals_), BF16)
    for step in range(locals_):
        whole = lax.dynamic_update_slice(
            whole, pieces[step], (0, source(locals_, me, step) * width)
        )
    gate = jnp.dot(whole[:cape], gate_w[0], preferred_element_type=F32)
    up = jnp.dot(whole[:cape], up_w[0], preferred_element_type=F32)
    d_hidden = lax.dot_general(whole[cape:], down_w[0], NT, preferred_element_type=F32)
    d_gate, d_up = hidden_terms(gate, up, d_hidden)
    partial = lax.dot_general(
        d_gate, gate_w[0], NT, preferred_element_type=F32
    ) + lax.dot_general(d_up, up_w[0], NT, preferred_element_type=F32)
    half = partial.astype(BF16)
    total = lax.dynamic_slice_in_dim(partial, me * width, width, 1)
    sent = [
        lax.dynamic_slice_in_dim(half, target(locals_, me, step) * width, width, 1)
        for step in range(1, locals_)
    ]
    for step in range(1, locals_):
        total = total + lax.ppermute(sent[step - 1], "local", partners(locals_, step)).astype(F32)
    d_rows = total.astype(BF16)

    back = lax.dot_general(
        sel, d_rows, (((0,), (0,)), ((), ())), preferred_element_type=F32
    ).astype(BF16)
    mine = lax.all_to_all(back.reshape(nodes, rows, width), "node", 0, 0, tiled=True)
    return jnp.sum(mine.astype(F32), axis=0).astype(BF16)


def column(width, index):
    return pl.ds(pl.multiple_of(index * width, width), width)


def place():
    return 2 * lax.axis_index("outer") + lax.axis_index("inner")


def block_terms(piece, cape, at, gate_ref, up_ref, down_ref):
    x, g = piece[:cape, :], piece[cape:, :]
    return (
        jnp.dot(x, gate_ref[at, :], preferred_element_type=F32),
        jnp.dot(x, up_ref[at, :], preferred_element_type=F32),
        lax.dot_general(g, down_ref[:, at], NT, preferred_element_type=F32),
    )


def first_kernel(cape, own, gate_hbm, up_hbm, down_hbm, acc, gate_ref, up_ref, down_ref, sems):
    me = place()
    width = own.shape[1]
    copies = []
    for step in range(4):
        at = column(width, me ^ step)
        copies.append(
            [
                pltpu.make_async_copy(gate_hbm.at[at, :], gate_ref.at[at, :], sems.at[0, step]),
                pltpu.make_async_copy(up_hbm.at[at, :], up_ref.at[at, :], sems.at[1, step]),
                pltpu.make_async_copy(down_hbm.at[:, at], down_ref.at[:, at], sems.at[2, step]),
            ]
        )
    for group in copies:
        for copy in group:
            copy.start()
    for copy in copies[0]:
        copy.wait()
    terms = block_terms(own, cape, column(width, me), gate_ref, up_ref, down_ref)
    for index, term in enumerate(terms):
        acc[index] = term
    for group in copies[1:]:
        for copy in group:
            copy.wait()


def third_kernel(cape, near, far, acc, gate_ref, up_ref, down_ref, out):
    me = place()
    width = near.shape[1]
    first = block_terms(near, cape, column(width, me ^ 1), gate_ref, up_ref, down_ref)
    second = block_terms(far, cape, column(width, me ^ 2), gate_ref, up_ref, down_ref)
    for index in range(3):
        out[index] = acc[index] + (first[index] + second[index])


def down_terms(d_gate, d_up, at, gate_ref, up_ref):
    return lax.dot_general(
        d_gate, gate_ref[at, :], NT, preferred_element_type=F32
    ) + lax.dot_general(d_up, up_ref[at, :], NT, preferred_element_type=F32)


def hidden_kernel(cape, piece, acc, gate_ref, up_ref, down_ref, sent, d_gate_ref, d_up_ref):
    me = place()
    width = piece.shape[1]
    terms = block_terms(piece, cape, column(width, me ^ 3), gate_ref, up_ref, down_ref)
    gate, up, d_hidden = [acc[index] + term for index, term in enumerate(terms)]
    d_gate, d_up = hidden_terms(gate, up, d_hidden)
    d_gate_ref[...] = d_gate
    d_up_ref[...] = d_up
    inner = (me & 1) ^ 1
    for outer in range(2):
        at = column(width, 2 * outer + inner)
        sent[:, outer * width : (outer + 1) * width] = down_terms(
            d_gate, d_up, at, gate_ref, up_ref
        ).astype(BF16)


def own_kernel(d_gate_ref, d_up_ref, gate_ref, up_ref, own):
    width = own.shape[1] // 2
    inner = place() & 1
    for outer in range(2):
        at = column(width, 2 * outer + inner)
        own[:, outer * width : (outer + 1) * width] = down_terms(
            d_gate_ref[...], d_up_ref[...], at, gate_ref, up_ref
        )


def call(body, outs, *args, hbm=(), scratch=(), limit=4, nbytes=1 << 18):
    args = [
        pltpu.with_memory_space_constraint(arg, pltpu.HBM) if index in hbm else arg
        for index, arg in enumerate(args)
    ]
    vmem = pl.BlockSpec(memory_space=pltpu.VMEM)
    far = pl.BlockSpec(memory_space=pltpu.HBM)
    return pl.pallas_call(
        body,
        out_shape=[jax.ShapeDtypeStruct(shape, dtype) for shape, dtype in outs],
        in_specs=[far if index in hbm else vmem for index in range(len(args))],
        out_specs=[vmem] * len(outs),
        scratch_shapes=list(scratch),
        compiler_params=pltpu.CompilerParams(vmem_limit_bytes=limit << 20),
        cost_estimate=pl.CostEstimate(flops=0, transcendentals=0, bytes_accessed=nbytes),
    )(*args)


def spread_kernel(
    cape, x_hbm, g_hbm, ids_hbm, probs_hbm, out, pick, factor, sel, x_ref, g_ref, ids_ref, probs_ref, sems
):
    pairs = ((ids_hbm, ids_ref), (probs_hbm, probs_ref), (x_hbm, x_ref), (g_hbm, g_ref))
    copies = [
        pltpu.make_async_copy(source_ref, there, sems.at[index])
        for index, (source_ref, there) in enumerate(pairs)
    ]
    for copy in copies:
        copy.start()
    nodes, block, _ = out.shape
    rows = block // 2
    tokens = ids_ref.shape[1]
    shift = block.bit_length() - 1

    def grid(height, width, axis):
        return lax.broadcasted_iota(jnp.int32, (height, width), axis)

    token = grid(tokens, nodes * block, 0)
    lane = grid(tokens, nodes * block, 1)
    held = (lane >> shift) * rows + (lane & (rows - 1))
    weight = jnp.concatenate(
        [
            (token < held).astype(BF16),
            (token == held).astype(BF16),
            (grid(tokens, tokens, 0) < grid(tokens, tokens, 1)).astype(BF16),
        ],
        axis=1,
    )
    slot = grid(2 * cape, nodes * block, 0)
    side = (grid(2 * cape, nodes * block, 1) & (block - 1)) >= rows
    wanted = jnp.where(side, slot - cape, slot).astype(F32)

    copies[0].wait()
    hit = ids_ref[...] == lax.axis_index("node")
    once = jnp.sum(jnp.where(hit, 1.0, 0.0), axis=0, keepdims=True)
    wide = jnp.broadcast_to(once, (8, tokens)).astype(BF16)
    counts = jnp.dot(wide, weight, preferred_element_type=F32)
    span = nodes * block
    there = jnp.where(counts[:1, span : 2 * span] > 0.5, counts[:1, :span], -2.0 * cape)
    pick[...] = jnp.where(there == wanted, 1.0, 0.0).astype(BF16)
    code = jnp.where(once > 0.5, counts[:1, 2 * span :], -2.0 * cape)
    mine = code == grid(cape, tokens, 0).astype(F32)
    sel[...] = jnp.where(mine, 1.0, 0.0).astype(BF16)
    copies[1].wait()
    scale = jnp.sum(jnp.where(hit, probs_ref[...], 0.0), axis=0, keepdims=True)
    factor[:cape, :] = jnp.ones((cape, 1), F32)
    factor[cape:, :] = jnp.sum(jnp.where(mine, scale, 0.0), axis=1, keepdims=True)
    copies[2].wait()
    copies[3].wait()
    for node in range(nodes):
        out[node, :rows, :] = x_ref[...]
        out[node, rows:, :] = g_ref[...]


def pick_kernel(pick, factor, every, own):
    part = jnp.dot(pick[...], every[...], preferred_element_type=F32)
    own[...] = (factor[...] * part).astype(BF16)


def shards(nodes, inputs, out_grad, expert_ids, route_probs, gate_w, up_w, down_w):
    gate_w, up_w, down_w = gate_w[0], up_w[0], down_w[0]
    rows, width = inputs.shape
    cape = 2 * rows * expert_ids.shape[1]
    swap = [(0, 1), (1, 0)]

    tokens = nodes * rows
    block, pick, factor, sel = call(
        functools.partial(spread_kernel, cape),
        [
            ((nodes, 2 * rows, width), BF16),
            ((2 * cape, 2 * tokens), BF16),
            ((2 * cape, 1), F32),
            ((cape, tokens), BF16),
        ],
        inputs, out_grad, expert_ids.T, route_probs.T,
        hbm=(0, 1, 2, 3),
        scratch=[
            pltpu.VMEM((rows, width), BF16),
            pltpu.VMEM((rows, width), BF16),
            pltpu.VMEM(expert_ids.shape[::-1], jnp.int32),
            pltpu.VMEM(route_probs.shape[::-1], F32),
            pltpu.SemaphoreType.DMA((4,)),
        ],
    )
    every = lax.all_to_all(block, "node", 0, 0, tiled=True)
    (own,) = call(
        pick_kernel,
        [((2 * cape, width), BF16)],
        pick, factor, every.reshape(2 * tokens, width),
    )
    far = lax.ppermute(own, "outer", swap)
    near = lax.ppermute(own, "inner", swap)
    hidden = down_w.shape[0]
    acc, gate_v, up_v, down_v = call(
        functools.partial(first_kernel, cape),
        [((3, cape, hidden), F32)] + [(w.shape, BF16) for w in (gate_w, up_w, down_w)],
        own, gate_w, up_w, down_w,
        hbm=(1, 2, 3),
        scratch=[pltpu.SemaphoreType.DMA((3, 4))],
        nbytes=6 << 20,
    )
    near, far, acc = lax.optimization_barrier((near, far, acc))
    across = lax.ppermute(far, "inner", swap)
    (acc,) = call(
        functools.partial(third_kernel, cape),
        [((3, cape, hidden), F32)],
        near, far, acc, gate_v, up_v, down_v,
    )
    sent, d_gate, d_up = call(
        functools.partial(hidden_kernel, cape),
        [((cape, 2 * width), BF16), ((cape, hidden), BF16), ((cape, hidden), BF16)],
        across, acc, gate_v, up_v, down_v,
    )
    got = lax.ppermute(sent, "inner", swap)
    (mine,) = call(own_kernel, [((cape, 2 * width), F32)], d_gate, d_up, gate_v, up_v)
    half = (mine + got.astype(F32)).astype(BF16)
    back = lax.dot_general(
        sel, half, (((0,), (0,)), ((), ())), preferred_element_type=F32
    ).astype(BF16)
    back = back.reshape(nodes, rows, 2, width).transpose(0, 2, 1, 3)
    home = lax.all_to_all(
        back.reshape(2 * nodes, rows, width), ("node", "outer"), 0, 0, tiled=True
    )
    return jnp.sum(home.astype(F32), axis=0).astype(BF16)


def solution(mesh):
    nodes, locals_ = mesh.shape["node"], mesh.shape["local"]

    def program(inputs, *args):
        width = inputs.shape[1] // locals_
        rows = inputs.shape[0] // nodes
        if locals_ == 4 and width % 128 == 0 and rows & (rows - 1) == 0:
            fine = jax.sharding.Mesh(
                mesh.devices.reshape(nodes, locals_ // 2, 2), ("node", "outer", "inner")
            )
            local = ("outer", "inner")
            body = functools.partial(shards, nodes)
        else:
            fine, local = mesh, "local"
            body = functools.partial(general, nodes, locals_)
        placed = (
            P("node", local),
            P("node", local),
            P(),
            P(),
            P("node", None, local),
            P("node", None, local),
            P("node", local, None),
        )
        return jax.shard_map(
            body, mesh=fine, in_specs=placed, out_specs=P("node", local), check_vma=False
        )(inputs, *args)

    return program
```

```python
import functools

import jax
import jax.numpy as jnp
from jax import lax
from jax.experimental import pallas as pl
from jax.experimental.pallas import tpu as pltpu
from jax.sharding import PartitionSpec as P

F32 = jnp.float32
BF16 = jnp.bfloat16
NT = (((1,), (1,)), ((), ()))


def slot_tables(expert_ids, route_probs, expert, cape):
    hit = expert_ids == expert
    tokens = expert_ids.shape[0]
    once = jnp.sum(hit.astype(F32), axis=1)
    scale = jnp.sum(jnp.where(hit, route_probs, 0.0), axis=1)
    row = lax.broadcasted_iota(jnp.int32, (tokens, tokens), 0)
    col = lax.broadcasted_iota(jnp.int32, (tokens, tokens), 1)
    rank = jnp.sum(jnp.where(col < row, once[None, :], 0.0), axis=1)
    slots = lax.broadcasted_iota(jnp.int32, (cape, tokens), 0).astype(F32)
    select = jnp.where((rank[None, :] == slots) & (once[None, :] > 0.5), 1.0, 0.0)
    return select, jnp.sum(select * scale[None, :], axis=1)


def partners(size, step):
    if size & (size - 1) == 0:
        return [(i, i ^ step) for i in range(size)]
    return [(i, (i + step) % size) for i in range(size)]


def source(size, me, step):
    if size & (size - 1) == 0:
        return me ^ step
    return lax.rem(me + (size - step), size)


def target(size, me, step):
    if size & (size - 1) == 0:
        return me ^ step
    return lax.rem(me + step, size)


def hidden_terms(gate, up, d_hidden):
    sig = jax.nn.sigmoid(gate)
    d_up = (d_hidden * (gate * sig)).astype(BF16)
    d_gate = (d_hidden * up * sig * (1.0 + gate * (1.0 - sig))).astype(BF16)
    return d_gate, d_up


def general(nodes, locals_, inputs, out_grad, expert_ids, route_probs, gate_w, up_w, down_w):
    expert = lax.axis_index("node")
    me = lax.axis_index("local")
    rows, width = inputs.shape
    cape = 2 * rows * expert_ids.shape[1]
    select, scale = slot_tables(expert_ids, route_probs, expert, cape)
    sel = select.astype(BF16)

    block = jnp.concatenate([inputs, out_grad], axis=0)
    every = lax.all_to_all(
        jnp.broadcast_to(block[None], (nodes,) + block.shape), "node", 0, 0, tiled=True
    )
    s3 = sel.reshape(cape, nodes, 1, rows)
    none = jnp.zeros_like(s3)
    pick = jnp.concatenate(
        [
            jnp.concatenate([s3, none], axis=2).reshape(cape, nodes * 2 * rows),
            jnp.concatenate([none, s3], axis=2).reshape(cape, nodes * 2 * rows),
        ],
        axis=0,
    )
    factor = jnp.concatenate([jnp.ones_like(scale), scale])
    part = jnp.dot(pick, every.reshape(nodes * 2 * rows, width), preferred_element_type=F32)
    part = (factor[:, None] * part).astype(BF16)

    pieces = [part] + [
        lax.ppermute(part, "local", partners(locals_, step)) for step in range(1, locals_)
    ]
    whole = jnp.zeros((2 * cape, width * locals_), BF16)
    for step in range(locals_):
        whole = lax.dynamic_update_slice(
            whole, pieces[step], (0, source(locals_, me, step) * width)
        )
    gate = jnp.dot(whole[:cape], gate_w[0], preferred_element_type=F32)
    up = jnp.dot(whole[:cape], up_w[0], preferred_element_type=F32)
    d_hidden = lax.dot_general(whole[cape:], down_w[0], NT, preferred_element_type=F32)
    d_gate, d_up = hidden_terms(gate, up, d_hidden)
    partial = lax.dot_general(
        d_gate, gate_w[0], NT, preferred_element_type=F32
    ) + lax.dot_general(d_up, up_w[0], NT, preferred_element_type=F32)
    half = partial.astype(BF16)
    total = lax.dynamic_slice_in_dim(partial, me * width, width, 1)
    sent = [
        lax.dynamic_slice_in_dim(half, target(locals_, me, step) * width, width, 1)
        for step in range(1, locals_)
    ]
    for step in range(1, locals_):
        total = total + lax.ppermute(sent[step - 1], "local", partners(locals_, step)).astype(F32)
    d_rows = total.astype(BF16)

    back = lax.dot_general(
        sel, d_rows, (((0,), (0,)), ((), ())), preferred_element_type=F32
    ).astype(BF16)
    mine = lax.all_to_all(back.reshape(nodes, rows, width), "node", 0, 0, tiled=True)
    return jnp.sum(mine.astype(F32), axis=0).astype(BF16)


def column(width, index):
    return pl.ds(pl.multiple_of(index * width, width), width)


def block_terms(piece, cape, at, gate_ref, up_ref, down_ref):
    x, g = piece[:cape, :], piece[cape:, :]
    return (
        jnp.dot(x, gate_ref[at, :], preferred_element_type=F32),
        jnp.dot(x, up_ref[at, :], preferred_element_type=F32),
        lax.dot_general(g, down_ref[:, at], NT, preferred_element_type=F32),
    )


def wide_terms(wide, cape, inner, gate_ref, up_ref, down_ref):
    width = wide.shape[1] // 2
    first, second = [
        block_terms(
            wide.at[:, pl.ds(outer * width, width)], cape, column(width, 2 * outer + inner),
            gate_ref, up_ref, down_ref,
        )
        for outer in range(2)
    ]
    return [a + b for a, b in zip(first, second)]


def third_kernel(cape, wide, gate_ref, up_ref, down_ref, out):
    terms = wide_terms(wide, cape, lax.axis_index("inner"), gate_ref, up_ref, down_ref)
    for index, term in enumerate(terms):
        out[index] = term


def down_terms(d_gate, d_up, at, gate_ref, up_ref):
    return lax.dot_general(
        d_gate, gate_ref[at, :], NT, preferred_element_type=F32
    ) + lax.dot_general(d_up, up_ref[at, :], NT, preferred_element_type=F32)


def hidden_kernel(cape, wide, acc, gate_ref, up_ref, down_ref, sent, d_gate_ref, d_up_ref):
    width = wide.shape[1] // 2
    inner = lax.axis_index("inner") ^ 1
    terms = wide_terms(wide, cape, inner, gate_ref, up_ref, down_ref)
    gate, up, d_hidden = [acc[index] + term for index, term in enumerate(terms)]
    d_gate, d_up = hidden_terms(gate, up, d_hidden)
    d_gate_ref[...] = d_gate
    d_up_ref[...] = d_up
    for outer in range(2):
        at = column(width, 2 * outer + inner)
        sent[:, outer * width : (outer + 1) * width] = down_terms(
            d_gate, d_up, at, gate_ref, up_ref
        ).astype(BF16)


def own_kernel(d_gate_ref, d_up_ref, gate_ref, up_ref, own):
    width = own.shape[1] // 2
    for outer in range(2):
        at = column(width, 2 * outer + lax.axis_index("inner"))
        own[:, outer * width : (outer + 1) * width] = down_terms(
            d_gate_ref[...], d_up_ref[...], at, gate_ref, up_ref
        )


def call(name, body, outs, *args, hbm=(), scratch=(), limit=4, nbytes=1 << 18):
    args = [
        pltpu.with_memory_space_constraint(arg, pltpu.HBM) if index in hbm else arg
        for index, arg in enumerate(args)
    ]
    vmem = pl.BlockSpec(memory_space=pltpu.VMEM)
    far = pl.BlockSpec(memory_space=pltpu.HBM)
    return pl.pallas_call(
        body,
        out_shape=[jax.ShapeDtypeStruct(shape, dtype) for shape, dtype in outs],
        in_specs=[far if index in hbm else vmem for index in range(len(args))],
        out_specs=[vmem] * len(outs),
        scratch_shapes=list(scratch),
        compiler_params=pltpu.CompilerParams(vmem_limit_bytes=limit << 20),
        cost_estimate=pl.CostEstimate(flops=0, transcendentals=0, bytes_accessed=nbytes),
        name=name,
    )(*args)


def prep_kernel(
    cape, half, rows, ids_hbm, probs_hbm, gate_hbm, up_hbm, down_hbm,
    pick, factor, sel, gate_ref, up_ref, down_ref, ids_ref, probs_ref, sems, weight_sems
):
    pairs = ((ids_hbm, ids_ref), (probs_hbm, probs_ref))
    copies = [
        pltpu.make_async_copy(source_ref, there, sems.at[index])
        for index, (source_ref, there) in enumerate(pairs)
    ]
    parts = weight_sems.shape[1]
    for index, (source_ref, there) in enumerate(
        ((gate_hbm, gate_ref), (up_hbm, up_ref), (down_hbm, down_ref))
    ):
        size = source_ref.shape[0] // parts
        for part in range(parts):
            at = pl.ds(part * size, size)
            copies.append(
                pltpu.make_async_copy(
                    source_ref.at[at, :], there.at[at, :], weight_sems.at[index, part]
                )
            )
    for copy in copies:
        copy.start()
    tokens = ids_ref.shape[1]
    block = 2 * rows
    span = pick.shape[1]

    def grid(height, width, axis):
        return lax.broadcasted_iota(jnp.int32, (height, width), axis)

    def held_of(lane):
        group = lane >> (2 * block).bit_length() - 1
        other = ((lane & block) != 0).astype(jnp.int32) ^ lax.axis_index("high")
        return (other * half + group) * rows + (lane & (rows - 1))

    token = grid(tokens, span, 0)
    held = held_of(grid(tokens, span, 1))
    weight = jnp.concatenate(
        [
            (token < held).astype(BF16),
            (token == held).astype(BF16),
            (grid(tokens, tokens, 0) < grid(tokens, tokens, 1)).astype(BF16),
        ],
        axis=1,
    )
    slot = grid(2 * cape, span, 0)
    side = (grid(2 * cape, span, 1) & rows) != 0
    wanted = jnp.where(side, slot - cape, slot).astype(F32)

    copies[0].wait()
    expert = lax.axis_index("high") * half + lax.axis_index("low")
    hit = ids_ref[...] == expert
    once = jnp.sum(jnp.where(hit, 1.0, 0.0), axis=0, keepdims=True)
    wide = jnp.broadcast_to(once, (8, tokens)).astype(BF16)
    counts = jnp.dot(wide, weight, preferred_element_type=F32)
    there = jnp.where(counts[:1, span : 2 * span] > 0.5, counts[:1, :span], -2.0 * cape)
    pick[...] = jnp.where(there == wanted, 1.0, 0.0).astype(BF16)
    code = jnp.where(once > 0.5, counts[:1, 2 * span :], -2.0 * cape)
    mine = code == grid(cape, tokens, 0).astype(F32)
    sel[...] = jnp.where(mine, 1.0, 0.0).astype(BF16)
    copies[1].wait()
    scale = jnp.sum(jnp.where(hit, probs_ref[...], 0.0), axis=0, keepdims=True)
    factor[:cape, :] = jnp.ones((cape, 1), F32)
    factor[cape:, :] = jnp.sum(jnp.where(mine, scale, 0.0), axis=1, keepdims=True)
    for copy in copies[2:]:
        copy.wait()


def join_kernel(x_hbm, g_hbm, out, sems):
    rows = x_hbm.shape[0]
    copies = [
        pltpu.make_async_copy(x_hbm, out.at[pl.ds(0, rows), :], sems.at[0]),
        pltpu.make_async_copy(g_hbm, out.at[pl.ds(rows, rows), :], sems.at[1]),
    ]
    for copy in copies:
        copy.start()
    for copy in copies:
        copy.wait()


def spread_kernel(near, far, out):
    rows = near.shape[0]
    for index in range(out.shape[0]):
        out[index, :rows, :] = near[...]
        out[index, rows:, :] = far[...]


def pick_kernel(pick, factor, every, wide):
    width = every.shape[2]
    for outer in range(2):
        part = jnp.dot(pick[...], every[outer], preferred_element_type=F32)
        wide[:, outer * width : (outer + 1) * width] = (factor[...] * part).astype(BF16)


def shards(nodes, inputs, out_grad, expert_ids, route_probs, gate_w, up_w, down_w):
    gate_w, up_w, down_w = gate_w[0], up_w[0], down_w[0]
    rows, width = inputs.shape
    cape = 2 * rows * expert_ids.shape[1]
    half = nodes // 2
    tokens = nodes * rows
    hidden = down_w.shape[0]
    swap = [(0, 1), (1, 0)]

    (near,) = call(
        "join",
        join_kernel,
        [((2 * rows, width), BF16)],
        inputs, out_grad,
        hbm=(0, 1),
        scratch=[pltpu.SemaphoreType.DMA((2,))],
    )
    far = lax.ppermute(near, "high", swap)
    pick, factor, sel, gate_v, up_v, down_v = call(
        "prep",
        functools.partial(prep_kernel, cape, half, rows),
        [
            ((2 * cape, 2 * tokens), BF16),
            ((2 * cape, 1), F32),
            ((cape, tokens), BF16),
        ]
        + [(w.shape, BF16) for w in (gate_w, up_w, down_w)],
        expert_ids.T, route_probs.T, gate_w, up_w, down_w,
        hbm=range(5),
        scratch=[
            pltpu.VMEM(expert_ids.shape[::-1], jnp.int32),
            pltpu.VMEM(route_probs.shape[::-1], F32),
            pltpu.SemaphoreType.DMA((2,)),
            pltpu.SemaphoreType.DMA((3, 4)),
        ],
        nbytes=6 << 20,
    )
    far, pick = lax.optimization_barrier((far, pick))
    (block,) = call("spread", spread_kernel, [((nodes, 4 * rows, width), BF16)], near, far)
    every = lax.all_to_all(block, ("outer", "low"), 0, 0, tiled=True)
    (wide,) = call(
        "pick",
        pick_kernel,
        [((2 * cape, 2 * width), BF16)],
        pick, factor, every.reshape(2, 2 * tokens, width),
    )
    across = lax.ppermute(wide, "inner", swap)
    (acc,) = call(
        "third",
        functools.partial(third_kernel, cape),
        [((3, cape, hidden), F32)],
        wide, gate_v, up_v, down_v,
    )
    across, acc = lax.optimization_barrier((across, acc))
    sent, d_gate, d_up = call(
        "hidden",
        functools.partial(hidden_kernel, cape),
        [((cape, 2 * width), BF16), ((cape, hidden), BF16), ((cape, hidden), BF16)],
        across, acc, gate_v, up_v, down_v,
    )
    got = lax.ppermute(sent, "inner", swap)
    (mine,) = call("own", own_kernel, [((cape, 2 * width), F32)], d_gate, d_up, gate_v, up_v)
    half = (mine + got.astype(F32)).astype(BF16)
    back = lax.dot_general(
        sel, half, (((0,), (0,)), ((), ())), preferred_element_type=F32
    ).astype(BF16)
    back = back.reshape(nodes, rows, 2, width).transpose(0, 2, 1, 3)
    home = lax.all_to_all(
        back.reshape(2 * nodes, rows, width), ("high", "low", "outer"), 0, 0, tiled=True
    )
    return jnp.sum(home.astype(F32), axis=0).astype(BF16)


def solution(mesh):
    nodes, locals_ = mesh.shape["node"], mesh.shape["local"]

    def program(inputs, *args):
        width = inputs.shape[1] // locals_
        rows = inputs.shape[0] // nodes
        if locals_ == 4 and width % 128 == 0 and nodes % 2 == 0 and rows & (rows - 1) == 0:
            fine = jax.sharding.Mesh(
                mesh.devices.reshape(2, nodes // 2, 2, 2), ("high", "low", "outer", "inner")
            )
            node, local = ("high", "low"), ("outer", "inner")
            body = functools.partial(shards, nodes)
        else:
            fine, node, local = mesh, "node", "local"
            body = functools.partial(general, nodes, locals_)
        placed = (
            P(node, local),
            P(node, local),
            P(),
            P(),
            P(node, None, local),
            P(node, None, local),
            P(node, local, None),
        )
        return jax.shard_map(
            body, mesh=fine, in_specs=placed, out_specs=P(node, local), check_vma=False
        )(inputs, *args)

    return program
```

```python
import functools

import jax
import jax.numpy as jnp
from jax import lax
from jax.experimental import pallas as pl
from jax.experimental.pallas import tpu as pltpu
from jax.sharding import PartitionSpec as P

F32 = jnp.float32
BF16 = jnp.bfloat16
NT = (((1,), (1,)), ((), ()))


def slot_tables(expert_ids, route_probs, expert, cape):
    hit = expert_ids == expert
    tokens = expert_ids.shape[0]
    once = jnp.sum(hit.astype(F32), axis=1)
    scale = jnp.sum(jnp.where(hit, route_probs, 0.0), axis=1)
    row = lax.broadcasted_iota(jnp.int32, (tokens, tokens), 0)
    col = lax.broadcasted_iota(jnp.int32, (tokens, tokens), 1)
    rank = jnp.sum(jnp.where(col < row, once[None, :], 0.0), axis=1)
    slots = lax.broadcasted_iota(jnp.int32, (cape, tokens), 0).astype(F32)
    select = jnp.where((rank[None, :] == slots) & (once[None, :] > 0.5), 1.0, 0.0)
    return select, jnp.sum(select * scale[None, :], axis=1)


def partners(size, step):
    if size & (size - 1) == 0:
        return [(i, i ^ step) for i in range(size)]
    return [(i, (i + step) % size) for i in range(size)]


def source(size, me, step):
    if size & (size - 1) == 0:
        return me ^ step
    return lax.rem(me + (size - step), size)


def target(size, me, step):
    if size & (size - 1) == 0:
        return me ^ step
    return lax.rem(me + step, size)


def hidden_terms(gate, up, d_hidden):
    sig = jax.nn.sigmoid(gate)
    d_up = (d_hidden * (gate * sig)).astype(BF16)
    d_gate = (d_hidden * up * sig * (1.0 + gate * (1.0 - sig))).astype(BF16)
    return d_gate, d_up


def general(nodes, locals_, inputs, out_grad, expert_ids, route_probs, gate_w, up_w, down_w):
    expert = lax.axis_index("node")
    me = lax.axis_index("local")
    rows, width = inputs.shape
    cape = 2 * rows * expert_ids.shape[1]
    select, scale = slot_tables(expert_ids, route_probs, expert, cape)
    sel = select.astype(BF16)

    block = jnp.concatenate([inputs, out_grad], axis=0)
    every = lax.all_to_all(
        jnp.broadcast_to(block[None], (nodes,) + block.shape), "node", 0, 0, tiled=True
    )
    s3 = sel.reshape(cape, nodes, 1, rows)
    none = jnp.zeros_like(s3)
    pick = jnp.concatenate(
        [
            jnp.concatenate([s3, none], axis=2).reshape(cape, nodes * 2 * rows),
            jnp.concatenate([none, s3], axis=2).reshape(cape, nodes * 2 * rows),
        ],
        axis=0,
    )
    factor = jnp.concatenate([jnp.ones_like(scale), scale])
    part = jnp.dot(pick, every.reshape(nodes * 2 * rows, width), preferred_element_type=F32)
    part = (factor[:, None] * part).astype(BF16)

    pieces = [part] + [
        lax.ppermute(part, "local", partners(locals_, step)) for step in range(1, locals_)
    ]
    whole = jnp.zeros((2 * cape, width * locals_), BF16)
    for step in range(locals_):
        whole = lax.dynamic_update_slice(
            whole, pieces[step], (0, source(locals_, me, step) * width)
        )
    gate = jnp.dot(whole[:cape], gate_w[0], preferred_element_type=F32)
    up = jnp.dot(whole[:cape], up_w[0], preferred_element_type=F32)
    d_hidden = lax.dot_general(whole[cape:], down_w[0], NT, preferred_element_type=F32)
    d_gate, d_up = hidden_terms(gate, up, d_hidden)
    partial = lax.dot_general(
        d_gate, gate_w[0], NT, preferred_element_type=F32
    ) + lax.dot_general(d_up, up_w[0], NT, preferred_element_type=F32)
    half = partial.astype(BF16)
    total = lax.dynamic_slice_in_dim(partial, me * width, width, 1)
    sent = [
        lax.dynamic_slice_in_dim(half, target(locals_, me, step) * width, width, 1)
        for step in range(1, locals_)
    ]
    for step in range(1, locals_):
        total = total + lax.ppermute(sent[step - 1], "local", partners(locals_, step)).astype(F32)
    d_rows = total.astype(BF16)

    back = lax.dot_general(
        sel, d_rows, (((0,), (0,)), ((), ())), preferred_element_type=F32
    ).astype(BF16)
    mine = lax.all_to_all(back.reshape(nodes, rows, width), "node", 0, 0, tiled=True)
    return jnp.sum(mine.astype(F32), axis=0).astype(BF16)


def column(width, index):
    return pl.ds(pl.multiple_of(index * width, width), width)


def block_terms(piece, cape, at, gate_ref, up_ref, down_ref):
    x, g = piece[:cape, :], piece[cape:, :]
    return (
        jnp.dot(x, gate_ref[at, :], preferred_element_type=F32),
        jnp.dot(x, up_ref[at, :], preferred_element_type=F32),
        lax.dot_general(g, down_ref[:, at], NT, preferred_element_type=F32),
    )


def wide_terms(wide, cape, inner, gate_ref, up_ref, down_ref):
    width = wide.shape[1] // 2
    first, second = [
        block_terms(
            wide.at[:, pl.ds(outer * width, width)], cape, column(width, 2 * outer + inner),
            gate_ref, up_ref, down_ref,
        )
        for outer in range(2)
    ]
    return [a + b for a, b in zip(first, second)]


def third_kernel(cape, wide, gate_ref, up_ref, down_ref, out):
    terms = wide_terms(wide, cape, lax.axis_index("inner"), gate_ref, up_ref, down_ref)
    for index, term in enumerate(terms):
        out[index] = term


def down_terms(d_gate, d_up, at, gate_ref, up_ref):
    return lax.dot_general(
        d_gate, gate_ref[at, :], NT, preferred_element_type=F32
    ) + lax.dot_general(d_up, up_ref[at, :], NT, preferred_element_type=F32)


def hidden_kernel(cape, wide, acc, gate_ref, up_ref, down_ref, sent, d_gate_ref, d_up_ref):
    width = wide.shape[1] // 2
    inner = lax.axis_index("inner") ^ 1
    terms = wide_terms(wide, cape, inner, gate_ref, up_ref, down_ref)
    gate, up, d_hidden = [acc[index] + term for index, term in enumerate(terms)]
    d_gate, d_up = hidden_terms(gate, up, d_hidden)
    d_gate_ref[...] = d_gate
    d_up_ref[...] = d_up
    for outer in range(2):
        at = column(width, 2 * outer + inner)
        sent[:, outer * width : (outer + 1) * width] = down_terms(
            d_gate, d_up, at, gate_ref, up_ref
        ).astype(BF16)


def own_kernel(d_gate_ref, d_up_ref, gate_ref, up_ref, own):
    width = own.shape[1] // 2
    for outer in range(2):
        at = column(width, 2 * outer + lax.axis_index("inner"))
        own[:, outer * width : (outer + 1) * width] = down_terms(
            d_gate_ref[...], d_up_ref[...], at, gate_ref, up_ref
        )


def call(name, body, outs, *args, hbm=(), scratch=(), limit=4, nbytes=1 << 18):
    args = [
        pltpu.with_memory_space_constraint(arg, pltpu.HBM) if index in hbm else arg
        for index, arg in enumerate(args)
    ]
    vmem = pl.BlockSpec(memory_space=pltpu.VMEM)
    far = pl.BlockSpec(memory_space=pltpu.HBM)
    return pl.pallas_call(
        body,
        out_shape=[jax.ShapeDtypeStruct(shape, dtype) for shape, dtype in outs],
        in_specs=[far if index in hbm else vmem for index in range(len(args))],
        out_specs=[vmem] * len(outs),
        scratch_shapes=list(scratch),
        compiler_params=pltpu.CompilerParams(vmem_limit_bytes=limit << 20),
        cost_estimate=pl.CostEstimate(flops=0, transcendentals=0, bytes_accessed=nbytes),
        name=name,
    )(*args)


def prep_kernel(
    cape, half, rows, ids_hbm, probs_hbm, gate_hbm, up_hbm, down_hbm,
    pick, factor, sel, gate_ref, up_ref, down_ref, ids_ref, probs_ref, sems, weight_sems
):
    pairs = ((ids_hbm, ids_ref), (probs_hbm, probs_ref))
    copies = [
        pltpu.make_async_copy(source_ref, there, sems.at[index])
        for index, (source_ref, there) in enumerate(pairs)
    ]
    parts = weight_sems.shape[1]
    for index, (source_ref, there) in enumerate(
        ((gate_hbm, gate_ref), (up_hbm, up_ref), (down_hbm, down_ref))
    ):
        size = source_ref.shape[0] // parts
        for part in range(parts):
            at = pl.ds(part * size, size)
            copies.append(
                pltpu.make_async_copy(
                    source_ref.at[at, :], there.at[at, :], weight_sems.at[index, part]
                )
            )
    for copy in copies:
        copy.start()
    tokens = ids_ref.shape[1]
    block = 2 * rows
    span = pick.shape[1]

    def grid(height, width, axis):
        return lax.broadcasted_iota(jnp.int32, (height, width), axis)

    def held_of(lane):
        group = lane >> (2 * block).bit_length() - 1
        other = ((lane & block) != 0).astype(jnp.int32) ^ lax.axis_index("high")
        return (other * half + group) * rows + (lane & (rows - 1))

    token = grid(tokens, span, 0)
    held = held_of(grid(tokens, span, 1))
    weight = jnp.concatenate(
        [
            (token < held).astype(BF16),
            (token == held).astype(BF16),
            (grid(tokens, tokens, 0) < grid(tokens, tokens, 1)).astype(BF16),
        ],
        axis=1,
    )
    slot = grid(2 * cape, span, 0)
    side = (grid(2 * cape, span, 1) & rows) != 0
    wanted = jnp.where(side, slot - cape, slot).astype(F32)

    copies[0].wait()
    expert = lax.axis_index("high") * half + lax.axis_index("low")
    hit = ids_ref[...] == expert
    once = jnp.sum(jnp.where(hit, 1.0, 0.0), axis=0, keepdims=True)
    wide = jnp.broadcast_to(once, (8, tokens)).astype(BF16)
    counts = jnp.dot(wide, weight, preferred_element_type=F32)
    there = jnp.where(counts[:1, span : 2 * span] > 0.5, counts[:1, :span], -2.0 * cape)
    pick[...] = jnp.where(there == wanted, 1.0, 0.0).astype(BF16)
    code = jnp.where(once > 0.5, counts[:1, 2 * span :], -2.0 * cape)
    mine = code == grid(cape, tokens, 0).astype(F32)
    sel[...] = jnp.where(mine, 1.0, 0.0).astype(BF16)
    copies[1].wait()
    scale = jnp.sum(jnp.where(hit, probs_ref[...], 0.0), axis=0, keepdims=True)
    factor[:cape, :] = jnp.ones((cape, 1), F32)
    factor[cape:, :] = jnp.sum(jnp.where(mine, scale, 0.0), axis=1, keepdims=True)
    for copy in copies[2:]:
        copy.wait()


def join_kernel(x_hbm, g_hbm, out, sems):
    rows = x_hbm.shape[0]
    copies = [
        pltpu.make_async_copy(x_hbm, out.at[pl.ds(0, rows), :], sems.at[0]),
        pltpu.make_async_copy(g_hbm, out.at[pl.ds(rows, rows), :], sems.at[1]),
    ]
    for copy in copies:
        copy.start()
    for copy in copies:
        copy.wait()


def spread_kernel(near, far, out):
    rows = near.shape[0]
    for index in range(out.shape[0]):
        out[index, :rows, :] = near[...]
        out[index, rows:, :] = far[...]


def pick_kernel(pick, factor, every, wide):
    width = every.shape[2]
    for outer in range(2):
        rows = jnp.concatenate([every[index] for index in range(outer, every.shape[0], 2)], axis=0)
        part = jnp.dot(pick[...], rows, preferred_element_type=F32)
        wide[:, outer * width : (outer + 1) * width] = (factor[...] * part).astype(BF16)


def shards(nodes, inputs, out_grad, expert_ids, route_probs, gate_w, up_w, down_w):
    gate_w, up_w, down_w = gate_w[0], up_w[0], down_w[0]
    rows, width = inputs.shape
    cape = 2 * rows * expert_ids.shape[1]
    half = nodes // 2
    tokens = nodes * rows
    hidden = down_w.shape[0]
    swap = [(0, 1), (1, 0)]

    (near,) = call(
        "join",
        join_kernel,
        [((2 * rows, width), BF16)],
        inputs, out_grad,
        hbm=(0, 1),
        scratch=[pltpu.SemaphoreType.DMA((2,))],
    )
    far = lax.ppermute(near, "high", swap)
    pick, factor, sel, gate_v, up_v, down_v = call(
        "prep",
        functools.partial(prep_kernel, cape, half, rows),
        [
            ((2 * cape, 2 * tokens), BF16),
            ((2 * cape, 1), F32),
            ((cape, tokens), BF16),
        ]
        + [(w.shape, BF16) for w in (gate_w, up_w, down_w)],
        expert_ids.T, route_probs.T, gate_w, up_w, down_w,
        hbm=range(5),
        scratch=[
            pltpu.VMEM(expert_ids.shape[::-1], jnp.int32),
            pltpu.VMEM(route_probs.shape[::-1], F32),
            pltpu.SemaphoreType.DMA((2,)),
            pltpu.SemaphoreType.DMA((3, 4)),
        ],
        nbytes=6 << 20,
    )
    far, pick = lax.optimization_barrier((far, pick))
    (block,) = call("spread", spread_kernel, [((nodes, 4 * rows, width), BF16)], near, far)
    every = lax.all_to_all(block, ("low", "outer"), 0, 0, tiled=True)
    (wide,) = call(
        "pick",
        pick_kernel,
        [((2 * cape, 2 * width), BF16)],
        pick, factor, every,
    )
    across = lax.ppermute(wide, "inner", swap)
    (acc,) = call(
        "third",
        functools.partial(third_kernel, cape),
        [((3, cape, hidden), F32)],
        wide, gate_v, up_v, down_v,
    )
    across, acc = lax.optimization_barrier((across, acc))
    sent, d_gate, d_up = call(
        "hidden",
        functools.partial(hidden_kernel, cape),
        [((cape, 2 * width), BF16), ((cape, hidden), BF16), ((cape, hidden), BF16)],
        across, acc, gate_v, up_v, down_v,
    )
    got = lax.ppermute(sent, "inner", swap)
    (mine,) = call("own", own_kernel, [((cape, 2 * width), F32)], d_gate, d_up, gate_v, up_v)
    half = (mine + got.astype(F32)).astype(BF16)
    back = lax.dot_general(
        sel, half, (((0,), (0,)), ((), ())), preferred_element_type=F32
    ).astype(BF16)
    back = back.reshape(nodes, rows, 2, width).transpose(0, 2, 1, 3)
    home = lax.all_to_all(
        back.reshape(2 * nodes, rows, width), ("high", "low", "outer"), 0, 0, tiled=True
    )
    return jnp.sum(home.astype(F32), axis=0).astype(BF16)


def solution(mesh):
    nodes, locals_ = mesh.shape["node"], mesh.shape["local"]

    def program(inputs, *args):
        width = inputs.shape[1] // locals_
        rows = inputs.shape[0] // nodes
        if locals_ == 4 and width % 128 == 0 and nodes % 2 == 0 and rows & (rows - 1) == 0:
            fine = jax.sharding.Mesh(
                mesh.devices.reshape(2, nodes // 2, 2, 2), ("high", "low", "outer", "inner")
            )
            node, local = ("high", "low"), ("outer", "inner")
            body = functools.partial(shards, nodes)
        else:
            fine, node, local = mesh, "node", "local"
            body = functools.partial(general, nodes, locals_)
        placed = (
            P(node, local),
            P(node, local),
            P(),
            P(),
            P(node, None, local),
            P(node, None, local),
            P(node, local, None),
        )
        return jax.shard_map(
            body, mesh=fine, in_specs=placed, out_specs=P(node, local), check_vma=False
        )(inputs, *args)

    return program
```

```python
import functools

import jax
import jax.numpy as jnp
from jax import lax
from jax.experimental import pallas as pl
from jax.experimental.pallas import tpu as pltpu
from jax.sharding import PartitionSpec as P

F32 = jnp.float32
BF16 = jnp.bfloat16
NT = (((1,), (1,)), ((), ()))
RETURN = ("low", "outer", "mid", "high")


def slot_of(half, node, outer):
    return ((((node % 2) * 2 + outer) * (half // 2) + node % half // 2) * 2 + node // half)


GATHER = ("mid", "low", "outer")


def source_of(half, node, outer):
    return (((node // 2) * 2 + node % 2) * 2 + outer)


def slot_tables(expert_ids, route_probs, expert, cape):
    hit = expert_ids == expert
    tokens = expert_ids.shape[0]
    once = jnp.sum(hit.astype(F32), axis=1)
    scale = jnp.sum(jnp.where(hit, route_probs, 0.0), axis=1)
    row = lax.broadcasted_iota(jnp.int32, (tokens, tokens), 0)
    col = lax.broadcasted_iota(jnp.int32, (tokens, tokens), 1)
    rank = jnp.sum(jnp.where(col < row, once[None, :], 0.0), axis=1)
    slots = lax.broadcasted_iota(jnp.int32, (cape, tokens), 0).astype(F32)
    select = jnp.where((rank[None, :] == slots) & (once[None, :] > 0.5), 1.0, 0.0)
    return select, jnp.sum(select * scale[None, :], axis=1)


def partners(size, step):
    if size & (size - 1) == 0:
        return [(i, i ^ step) for i in range(size)]
    return [(i, (i + step) % size) for i in range(size)]


def source(size, me, step):
    if size & (size - 1) == 0:
        return me ^ step
    return lax.rem(me + (size - step), size)


def target(size, me, step):
    if size & (size - 1) == 0:
        return me ^ step
    return lax.rem(me + step, size)


def hidden_terms(gate, up, d_hidden):
    sig = jax.nn.sigmoid(gate)
    d_up = (d_hidden * (gate * sig)).astype(BF16)
    d_gate = (d_hidden * up * sig * (1.0 + gate * (1.0 - sig))).astype(BF16)
    return d_gate, d_up


def general(nodes, locals_, inputs, out_grad, expert_ids, route_probs, gate_w, up_w, down_w):
    expert = lax.axis_index("node")
    me = lax.axis_index("local")
    rows, width = inputs.shape
    cape = 2 * rows * expert_ids.shape[1]
    select, scale = slot_tables(expert_ids, route_probs, expert, cape)
    sel = select.astype(BF16)

    block = jnp.concatenate([inputs, out_grad], axis=0)
    every = lax.all_to_all(
        jnp.broadcast_to(block[None], (nodes,) + block.shape), "node", 0, 0, tiled=True
    )
    s3 = sel.reshape(cape, nodes, 1, rows)
    none = jnp.zeros_like(s3)
    pick = jnp.concatenate(
        [
            jnp.concatenate([s3, none], axis=2).reshape(cape, nodes * 2 * rows),
            jnp.concatenate([none, s3], axis=2).reshape(cape, nodes * 2 * rows),
        ],
        axis=0,
    )
    factor = jnp.concatenate([jnp.ones_like(scale), scale])
    part = jnp.dot(pick, every.reshape(nodes * 2 * rows, width), preferred_element_type=F32)
    part = (factor[:, None] * part).astype(BF16)

    pieces = [part] + [
        lax.ppermute(part, "local", partners(locals_, step)) for step in range(1, locals_)
    ]
    whole = jnp.zeros((2 * cape, width * locals_), BF16)
    for step in range(locals_):
        whole = lax.dynamic_update_slice(
            whole, pieces[step], (0, source(locals_, me, step) * width)
        )
    gate = jnp.dot(whole[:cape], gate_w[0], preferred_element_type=F32)
    up = jnp.dot(whole[:cape], up_w[0], preferred_element_type=F32)
    d_hidden = lax.dot_general(whole[cape:], down_w[0], NT, preferred_element_type=F32)
    d_gate, d_up = hidden_terms(gate, up, d_hidden)
    partial = lax.dot_general(
        d_gate, gate_w[0], NT, preferred_element_type=F32
    ) + lax.dot_general(d_up, up_w[0], NT, preferred_element_type=F32)
    half = partial.astype(BF16)
    total = lax.dynamic_slice_in_dim(partial, me * width, width, 1)
    sent = [
        lax.dynamic_slice_in_dim(half, target(locals_, me, step) * width, width, 1)
        for step in range(1, locals_)
    ]
    for step in range(1, locals_):
        total = total + lax.ppermute(sent[step - 1], "local", partners(locals_, step)).astype(F32)
    d_rows = total.astype(BF16)

    back = lax.dot_general(
        sel, d_rows, (((0,), (0,)), ((), ())), preferred_element_type=F32
    ).astype(BF16)
    mine = lax.all_to_all(back.reshape(nodes, rows, width), "node", 0, 0, tiled=True)
    return jnp.sum(mine.astype(F32), axis=0).astype(BF16)


def column(width, index):
    return pl.ds(pl.multiple_of(index * width, width), width)


def block_terms(piece, cape, at, gate_ref, up_ref, down_ref):
    x, g = piece[:cape, :], piece[cape:, :]
    return (
        jnp.dot(x, gate_ref[at, :], preferred_element_type=F32),
        jnp.dot(x, up_ref[at, :], preferred_element_type=F32),
        lax.dot_general(g, down_ref[:, at], NT, preferred_element_type=F32),
    )


def wide_terms(wide, cape, inner, gate_ref, up_ref, down_ref):
    width = wide.shape[1] // 2
    first, second = [
        block_terms(
            wide.at[:, pl.ds(outer * width, width)], cape, column(width, 2 * outer + inner),
            gate_ref, up_ref, down_ref,
        )
        for outer in range(2)
    ]
    return [a + b for a, b in zip(first, second)]


def third_kernel(cape, wide, gate_ref, up_ref, down_ref, out):
    terms = wide_terms(wide, cape, lax.axis_index("inner"), gate_ref, up_ref, down_ref)
    for index, term in enumerate(terms):
        out[index] = term


def down_terms(d_gate, d_up, at, gate_ref, up_ref):
    return lax.dot_general(
        d_gate, gate_ref[at, :], NT, preferred_element_type=F32
    ) + lax.dot_general(d_up, up_ref[at, :], NT, preferred_element_type=F32)


def hidden_kernel(cape, wide, acc, gate_ref, up_ref, down_ref, sent, d_gate_ref, d_up_ref):
    width = wide.shape[1] // 2
    inner = lax.axis_index("inner") ^ 1
    terms = wide_terms(wide, cape, inner, gate_ref, up_ref, down_ref)
    gate, up, d_hidden = [acc[index] + term for index, term in enumerate(terms)]
    d_gate, d_up = hidden_terms(gate, up, d_hidden)
    d_gate_ref[...] = d_gate
    d_up_ref[...] = d_up
    for outer in range(2):
        at = column(width, 2 * outer + inner)
        sent[:, outer * width : (outer + 1) * width] = down_terms(
            d_gate, d_up, at, gate_ref, up_ref
        ).astype(BF16)


def own_kernel(d_gate_ref, d_up_ref, gate_ref, up_ref, own):
    width = own.shape[1] // 2
    for outer in range(2):
        at = column(width, 2 * outer + lax.axis_index("inner"))
        own[:, outer * width : (outer + 1) * width] = down_terms(
            d_gate_ref[...], d_up_ref[...], at, gate_ref, up_ref
        )


def call(name, body, outs, *args, hbm=(), scratch=(), limit=4, nbytes=1 << 18):
    args = [
        pltpu.with_memory_space_constraint(arg, pltpu.HBM) if index in hbm else arg
        for index, arg in enumerate(args)
    ]
    vmem = pl.BlockSpec(memory_space=pltpu.VMEM)
    far = pl.BlockSpec(memory_space=pltpu.HBM)
    return pl.pallas_call(
        body,
        out_shape=[jax.ShapeDtypeStruct(shape, dtype) for shape, dtype in outs],
        in_specs=[far if index in hbm else vmem for index in range(len(args))],
        out_specs=[vmem] * len(outs),
        scratch_shapes=list(scratch),
        compiler_params=pltpu.CompilerParams(vmem_limit_bytes=limit << 20),
        cost_estimate=pl.CostEstimate(flops=0, transcendentals=0, bytes_accessed=nbytes),
        name=name,
    )(*args)


def prep_kernel(
    cape, half, rows, ids_hbm, probs_hbm, gate_hbm, up_hbm, down_hbm,
    pick, factor, sel, gate_ref, up_ref, down_ref, ids_ref, probs_ref, sems, weight_sems
):
    pairs = ((ids_hbm, ids_ref), (probs_hbm, probs_ref))
    copies = [
        pltpu.make_async_copy(source_ref, there, sems.at[index])
        for index, (source_ref, there) in enumerate(pairs)
    ]
    parts = weight_sems.shape[1]
    for index, (source_ref, there) in enumerate(
        ((gate_hbm, gate_ref), (up_hbm, up_ref), (down_hbm, down_ref))
    ):
        size = source_ref.shape[0] // parts
        for part in range(parts):
            at = pl.ds(part * size, size)
            copies.append(
                pltpu.make_async_copy(
                    source_ref.at[at, :], there.at[at, :], weight_sems.at[index, part]
                )
            )
    for copy in copies:
        copy.start()
    tokens = ids_ref.shape[1]
    block = 2 * rows
    span = pick.shape[1]

    def grid(height, width, axis):
        return lax.broadcasted_iota(jnp.int32, (height, width), axis)

    def held_of(lane):
        group = lane >> (2 * block).bit_length() - 1
        other = ((lane & block) != 0).astype(jnp.int32) ^ lax.axis_index("high")
        return (other * half + group) * rows + (lane & (rows - 1))

    token = grid(tokens, span, 0)
    held = held_of(grid(tokens, span, 1))
    weight = jnp.concatenate(
        [
            (token < held).astype(BF16),
            (token == held).astype(BF16),
            (grid(tokens, tokens, 0) < grid(tokens, tokens, 1)).astype(BF16),
        ],
        axis=1,
    )
    slot = grid(2 * cape, span, 0)
    side = (grid(2 * cape, span, 1) & rows) != 0
    wanted = jnp.where(side, slot - cape, slot).astype(F32)

    copies[0].wait()
    expert = lax.axis_index("high") * half + 2 * lax.axis_index("mid") + lax.axis_index("low")
    hit = ids_ref[...] == expert
    once = jnp.sum(jnp.where(hit, 1.0, 0.0), axis=0, keepdims=True)
    wide = jnp.broadcast_to(once, (8, tokens)).astype(BF16)
    counts = jnp.dot(wide, weight, preferred_element_type=F32)
    there = jnp.where(counts[:1, span : 2 * span] > 0.5, counts[:1, :span], -2.0 * cape)
    pick[...] = jnp.where(there == wanted, 1.0, 0.0).astype(BF16)
    code = jnp.where(once > 0.5, counts[:1, 2 * span :], -2.0 * cape)
    mine = code == grid(cape, tokens, 0).astype(F32)
    sel[...] = jnp.where(mine, 1.0, 0.0).astype(BF16)
    copies[1].wait()
    scale = jnp.sum(jnp.where(hit, probs_ref[...], 0.0), axis=0, keepdims=True)
    factor[:cape, :] = jnp.ones((cape, 1), F32)
    factor[cape:, :] = jnp.sum(jnp.where(mine, scale, 0.0), axis=1, keepdims=True)
    for copy in copies[2:]:
        copy.wait()


def join_kernel(x_hbm, g_hbm, out, sems):
    rows = x_hbm.shape[0]
    copies = [
        pltpu.make_async_copy(x_hbm, out.at[pl.ds(0, rows), :], sems.at[0]),
        pltpu.make_async_copy(g_hbm, out.at[pl.ds(rows, rows), :], sems.at[1]),
    ]
    for copy in copies:
        copy.start()
    for copy in copies:
        copy.wait()


def spread_kernel(near, far, out):
    rows = near.shape[0]
    for index in range(out.shape[0]):
        out[index, :rows, :] = near[...]
        out[index, rows:, :] = far[...]


def scatter_kernel(rows, sel, mine, got, out):
    half = (mine[...] + got[...].astype(F32)).astype(BF16)
    back = lax.dot_general(
        sel[...], half, (((0,), (0,)), ((), ())), preferred_element_type=F32
    ).astype(BF16)
    width = out.shape[2]
    nodes = out.shape[0] // 2
    for node in range(nodes):
        for outer in range(2):
            out[slot_of(nodes // 2, node, outer)] = back[
                node * rows : (node + 1) * rows, outer * width : (outer + 1) * width
            ]


def pick_kernel(pick, factor, every, wide):
    width = every.shape[2]
    half = every.shape[0] // 2
    for outer in range(2):
        rows = jnp.concatenate(
            [every[source_of(half, node, outer)] for node in range(half)], axis=0
        )
        part = jnp.dot(pick[...], rows, preferred_element_type=F32)
        wide[:, outer * width : (outer + 1) * width] = (factor[...] * part).astype(BF16)


def shards(nodes, inputs, out_grad, expert_ids, route_probs, gate_w, up_w, down_w):
    gate_w, up_w, down_w = gate_w[0], up_w[0], down_w[0]
    rows, width = inputs.shape
    cape = 2 * rows * expert_ids.shape[1]
    half = nodes // 2
    tokens = nodes * rows
    hidden = down_w.shape[0]
    swap = [(0, 1), (1, 0)]

    (near,) = call(
        "join",
        join_kernel,
        [((2 * rows, width), BF16)],
        inputs, out_grad,
        hbm=(0, 1),
        scratch=[pltpu.SemaphoreType.DMA((2,))],
    )
    far = lax.ppermute(near, "high", swap)
    pick, factor, sel, gate_v, up_v, down_v = call(
        "prep",
        functools.partial(prep_kernel, cape, half, rows),
        [
            ((2 * cape, 2 * tokens), BF16),
            ((2 * cape, 1), F32),
            ((cape, tokens), BF16),
        ]
        + [(w.shape, BF16) for w in (gate_w, up_w, down_w)],
        expert_ids.T, route_probs.T, gate_w, up_w, down_w,
        hbm=range(5),
        scratch=[
            pltpu.VMEM(expert_ids.shape[::-1], jnp.int32),
            pltpu.VMEM(route_probs.shape[::-1], F32),
            pltpu.SemaphoreType.DMA((2,)),
            pltpu.SemaphoreType.DMA((3, 4)),
        ],
        nbytes=6 << 20,
    )
    far, pick = lax.optimization_barrier((far, pick))
    (block,) = call("spread", spread_kernel, [((nodes, 4 * rows, width), BF16)], near, far)
    every = lax.all_to_all(block, GATHER, 0, 0, tiled=True)
    (wide,) = call(
        "pick",
        pick_kernel,
        [((2 * cape, 2 * width), BF16)],
        pick, factor, every,
    )
    across = lax.ppermute(wide, "inner", swap)
    (acc,) = call(
        "third",
        functools.partial(third_kernel, cape),
        [((3, cape, hidden), F32)],
        wide, gate_v, up_v, down_v,
    )
    across, acc = lax.optimization_barrier((across, acc))
    sent, d_gate, d_up = call(
        "hidden",
        functools.partial(hidden_kernel, cape),
        [((cape, 2 * width), BF16), ((cape, hidden), BF16), ((cape, hidden), BF16)],
        across, acc, gate_v, up_v, down_v,
    )
    got = lax.ppermute(sent, "inner", swap)
    (mine,) = call("own", own_kernel, [((cape, 2 * width), F32)], d_gate, d_up, gate_v, up_v)
    (back,) = call(
        "scatter",
        functools.partial(scatter_kernel, rows),
        [((2 * nodes, rows, width), BF16)],
        sel, mine, got,
    )
    home = lax.all_to_all(back, RETURN, 0, 0, tiled=True)
    return jnp.sum(home.astype(F32), axis=0).astype(BF16)


def solution(mesh):
    nodes, locals_ = mesh.shape["node"], mesh.shape["local"]

    def program(inputs, *args):
        width = inputs.shape[1] // locals_
        rows = inputs.shape[0] // nodes
        if locals_ == 4 and width % 128 == 0 and nodes % 4 == 0 and rows & (rows - 1) == 0:
            fine = jax.sharding.Mesh(
                mesh.devices.reshape(2, nodes // 4, 2, 2, 2), ("high", "mid", "low", "outer", "inner")
            )
            node, local = ("high", "mid", "low"), ("outer", "inner")
            body = functools.partial(shards, nodes)
        else:
            fine, node, local = mesh, "node", "local"
            body = functools.partial(general, nodes, locals_)
        placed = (
            P(node, local),
            P(node, local),
            P(),
            P(),
            P(node, None, local),
            P(node, None, local),
            P(node, local, None),
        )
        return jax.shard_map(
            body, mesh=fine, in_specs=placed, out_specs=P(node, local), check_vma=False
        )(inputs, *args)

    return program
```

```python
import functools

import jax
import jax.numpy as jnp
from jax import lax
from jax.experimental import pallas as pl
from jax.experimental.pallas import tpu as pltpu
from jax.sharding import PartitionSpec as P

F32 = jnp.float32
BF16 = jnp.bfloat16
NT = (((1,), (1,)), ((), ()))
RETURN = ("low", "outer", "mid", "high")


def slot_of(half, node, outer):
    return ((((node % 2) * 2 + outer) * (half // 2) + node % half // 2) * 2 + node // half)


GATHER = ("mid", "low", "outer")


def source_of(half, node, outer):
    return (((node // 2) * 2 + node % 2) * 2 + outer)


def slot_tables(expert_ids, route_probs, expert, cape):
    hit = expert_ids == expert
    tokens = expert_ids.shape[0]
    once = jnp.sum(hit.astype(F32), axis=1)
    scale = jnp.sum(jnp.where(hit, route_probs, 0.0), axis=1)
    row = lax.broadcasted_iota(jnp.int32, (tokens, tokens), 0)
    col = lax.broadcasted_iota(jnp.int32, (tokens, tokens), 1)
    rank = jnp.sum(jnp.where(col < row, once[None, :], 0.0), axis=1)
    slots = lax.broadcasted_iota(jnp.int32, (cape, tokens), 0).astype(F32)
    select = jnp.where((rank[None, :] == slots) & (once[None, :] > 0.5), 1.0, 0.0)
    return select, jnp.sum(select * scale[None, :], axis=1)


def partners(size, step):
    if size & (size - 1) == 0:
        return [(i, i ^ step) for i in range(size)]
    return [(i, (i + step) % size) for i in range(size)]


def source(size, me, step):
    if size & (size - 1) == 0:
        return me ^ step
    return lax.rem(me + (size - step), size)


def target(size, me, step):
    if size & (size - 1) == 0:
        return me ^ step
    return lax.rem(me + step, size)


def hidden_terms(gate, up, d_hidden):
    sig = jax.nn.sigmoid(gate)
    d_up = (d_hidden * (gate * sig)).astype(BF16)
    d_gate = (d_hidden * up * sig * (1.0 + gate * (1.0 - sig))).astype(BF16)
    return d_gate, d_up


def general(nodes, locals_, inputs, out_grad, expert_ids, route_probs, gate_w, up_w, down_w):
    expert = lax.axis_index("node")
    me = lax.axis_index("local")
    rows, width = inputs.shape
    cape = 2 * rows * expert_ids.shape[1]
    select, scale = slot_tables(expert_ids, route_probs, expert, cape)
    sel = select.astype(BF16)

    block = jnp.concatenate([inputs, out_grad], axis=0)
    every = lax.all_to_all(
        jnp.broadcast_to(block[None], (nodes,) + block.shape), "node", 0, 0, tiled=True
    )
    s3 = sel.reshape(cape, nodes, 1, rows)
    none = jnp.zeros_like(s3)
    pick = jnp.concatenate(
        [
            jnp.concatenate([s3, none], axis=2).reshape(cape, nodes * 2 * rows),
            jnp.concatenate([none, s3], axis=2).reshape(cape, nodes * 2 * rows),
        ],
        axis=0,
    )
    factor = jnp.concatenate([jnp.ones_like(scale), scale])
    part = jnp.dot(pick, every.reshape(nodes * 2 * rows, width), preferred_element_type=F32)
    part = (factor[:, None] * part).astype(BF16)

    pieces = [part] + [
        lax.ppermute(part, "local", partners(locals_, step)) for step in range(1, locals_)
    ]
    whole = jnp.zeros((2 * cape, width * locals_), BF16)
    for step in range(locals_):
        whole = lax.dynamic_update_slice(
            whole, pieces[step], (0, source(locals_, me, step) * width)
        )
    gate = jnp.dot(whole[:cape], gate_w[0], preferred_element_type=F32)
    up = jnp.dot(whole[:cape], up_w[0], preferred_element_type=F32)
    d_hidden = lax.dot_general(whole[cape:], down_w[0], NT, preferred_element_type=F32)
    d_gate, d_up = hidden_terms(gate, up, d_hidden)
    partial = lax.dot_general(
        d_gate, gate_w[0], NT, preferred_element_type=F32
    ) + lax.dot_general(d_up, up_w[0], NT, preferred_element_type=F32)
    half = partial.astype(BF16)
    total = lax.dynamic_slice_in_dim(partial, me * width, width, 1)
    sent = [
        lax.dynamic_slice_in_dim(half, target(locals_, me, step) * width, width, 1)
        for step in range(1, locals_)
    ]
    for step in range(1, locals_):
        total = total + lax.ppermute(sent[step - 1], "local", partners(locals_, step)).astype(F32)
    d_rows = total.astype(BF16)

    back = lax.dot_general(
        sel, d_rows, (((0,), (0,)), ((), ())), preferred_element_type=F32
    ).astype(BF16)
    mine = lax.all_to_all(back.reshape(nodes, rows, width), "node", 0, 0, tiled=True)
    return jnp.sum(mine.astype(F32), axis=0).astype(BF16)


def column(width, index):
    return pl.ds(pl.multiple_of(index * width, width), width)


def block_terms(piece, cape, at, gate_ref, up_ref, down_ref):
    x, g = piece[:cape, :], piece[cape:, :]
    grad = lax.dot_general(g, down_ref[:, at], NT, preferred_element_type=F32)
    return (
        jnp.dot(x, gate_ref[at, :], preferred_element_type=F32),
        jnp.dot(x, up_ref[at, :], preferred_element_type=F32),
        grad,
    )


def wide_terms(wide, cape, inner, gate_ref, up_ref, down_ref):
    width = wide.shape[1] // 2
    places = [column(width, 2 * outer + inner) for outer in range(2)]
    xs = [wide[:cape, outer * width : (outer + 1) * width] for outer in range(2)]
    gs = [wide[cape:, outer * width : (outer + 1) * width] for outer in range(2)]
    grad = [
        lax.dot_general(g, down_ref[:, at], NT, preferred_element_type=F32)
        for g, at in zip(gs, places)
    ]
    gate = [jnp.dot(x, gate_ref[at, :], preferred_element_type=F32) for x, at in zip(xs, places)]
    up = [jnp.dot(x, up_ref[at, :], preferred_element_type=F32) for x, at in zip(xs, places)]
    return gate[0] + gate[1], up[0] + up[1], grad[0] + grad[1]


def third_kernel(cape, wide, gate_ref, up_ref, down_ref, out):
    terms = wide_terms(wide, cape, lax.axis_index("inner"), gate_ref, up_ref, down_ref)
    for index, term in enumerate(terms):
        out[index] = term


def down_terms(d_gate, d_up, at, gate_ref, up_ref):
    return lax.dot_general(
        d_gate, gate_ref[at, :], NT, preferred_element_type=F32
    ) + lax.dot_general(d_up, up_ref[at, :], NT, preferred_element_type=F32)


def hidden_kernel(cape, wide, acc, gate_ref, up_ref, down_ref, sent, d_gate_ref, d_up_ref):
    width = wide.shape[1] // 2
    inner = lax.axis_index("inner") ^ 1
    terms = wide_terms(wide, cape, inner, gate_ref, up_ref, down_ref)
    gate, up, d_hidden = [acc[index] + term for index, term in enumerate(terms)]
    d_gate, d_up = hidden_terms(gate, up, d_hidden)
    d_gate_ref[...] = d_gate
    d_up_ref[...] = d_up
    for outer in range(2):
        at = column(width, 2 * outer + inner)
        sent[:, outer * width : (outer + 1) * width] = down_terms(
            d_gate, d_up, at, gate_ref, up_ref
        ).astype(BF16)


def own_kernel(d_gate_ref, d_up_ref, gate_ref, up_ref, own):
    width = own.shape[1] // 2
    for outer in range(2):
        at = column(width, 2 * outer + lax.axis_index("inner"))
        own[:, outer * width : (outer + 1) * width] = down_terms(
            d_gate_ref[...], d_up_ref[...], at, gate_ref, up_ref
        )


def call(name, body, outs, *args, hbm=(), scratch=(), limit=4, nbytes=1 << 18):
    args = [
        pltpu.with_memory_space_constraint(arg, pltpu.HBM) if index in hbm else arg
        for index, arg in enumerate(args)
    ]
    vmem = pl.BlockSpec(memory_space=pltpu.VMEM)
    far = pl.BlockSpec(memory_space=pltpu.HBM)
    return pl.pallas_call(
        body,
        out_shape=[jax.ShapeDtypeStruct(shape, dtype) for shape, dtype in outs],
        in_specs=[far if index in hbm else vmem for index in range(len(args))],
        out_specs=[vmem] * len(outs),
        scratch_shapes=list(scratch),
        compiler_params=pltpu.CompilerParams(vmem_limit_bytes=limit << 20),
        cost_estimate=pl.CostEstimate(flops=0, transcendentals=0, bytes_accessed=nbytes),
        name=name,
    )(*args)


def prep_kernel(
    cape, half, rows, ids_hbm, probs_hbm, gate_hbm, up_hbm, down_hbm,
    pick, factor, sel, gate_ref, up_ref, down_ref, ids_ref, probs_ref, sems, weight_sems
):
    pairs = ((ids_hbm, ids_ref), (probs_hbm, probs_ref))
    copies = [
        pltpu.make_async_copy(source_ref, there, sems.at[index])
        for index, (source_ref, there) in enumerate(pairs)
    ]
    parts = weight_sems.shape[1]
    for index, (source_ref, there) in enumerate(
        ((gate_hbm, gate_ref), (up_hbm, up_ref), (down_hbm, down_ref))
    ):
        size = source_ref.shape[0] // parts
        for part in range(parts):
            at = pl.ds(part * size, size)
            copies.append(
                pltpu.make_async_copy(
                    source_ref.at[at, :], there.at[at, :], weight_sems.at[index, part]
                )
            )
    for copy in copies:
        copy.start()
    tokens = ids_ref.shape[1]
    block = 2 * rows
    span = pick.shape[1]

    def grid(height, width, axis):
        return lax.broadcasted_iota(jnp.int32, (height, width), axis)

    def held_of(lane):
        group = lane >> (2 * block).bit_length() - 1
        other = ((lane & block) != 0).astype(jnp.int32) ^ lax.axis_index("high")
        return (other * half + group) * rows + (lane & (rows - 1))

    token = grid(tokens, span, 0)
    held = held_of(grid(tokens, span, 1))
    weight = jnp.concatenate(
        [
            (token < held).astype(BF16),
            (token == held).astype(BF16),
            (grid(tokens, tokens, 0) < grid(tokens, tokens, 1)).astype(BF16),
        ],
        axis=1,
    )
    slot = grid(2 * cape, span, 0)
    side = (grid(2 * cape, span, 1) & rows) != 0
    wanted = jnp.where(side, slot - cape, slot).astype(F32)

    copies[0].wait()
    expert = lax.axis_index("high") * half + 2 * lax.axis_index("mid") + lax.axis_index("low")
    hit = ids_ref[...] == expert
    once = jnp.sum(jnp.where(hit, 1.0, 0.0), axis=0, keepdims=True)
    wide = jnp.broadcast_to(once, (8, tokens)).astype(BF16)
    counts = jnp.dot(wide, weight, preferred_element_type=F32)
    there = jnp.where(counts[:1, span : 2 * span] > 0.5, counts[:1, :span], -2.0 * cape)
    pick[...] = jnp.where(there == wanted, 1.0, 0.0).astype(BF16)
    code = jnp.where(once > 0.5, counts[:1, 2 * span :], -2.0 * cape)
    mine = code == grid(cape, tokens, 0).astype(F32)
    sel[...] = jnp.where(mine, 1.0, 0.0).astype(BF16)
    copies[1].wait()
    scale = jnp.sum(jnp.where(hit, probs_ref[...], 0.0), axis=0, keepdims=True)
    factor[:cape, :] = jnp.ones((cape, 1), F32)
    factor[cape:, :] = jnp.sum(jnp.where(mine, scale, 0.0), axis=1, keepdims=True)
    for copy in copies[2:]:
        copy.wait()


def join_kernel(x_hbm, g_hbm, out, sems):
    rows = x_hbm.shape[0]
    copies = [
        pltpu.make_async_copy(x_hbm, out.at[pl.ds(0, rows), :], sems.at[0]),
        pltpu.make_async_copy(g_hbm, out.at[pl.ds(rows, rows), :], sems.at[1]),
    ]
    for copy in copies:
        copy.start()
    for copy in copies:
        copy.wait()


def spread_kernel(near, far, out):
    rows = near.shape[0]
    for index in range(out.shape[0]):
        out[index, :rows, :] = near[...]
        out[index, rows:, :] = far[...]


def scatter_kernel(rows, sel, mine, got, out):
    half = (mine[...] + got[...].astype(F32)).astype(BF16)
    back = lax.dot_general(
        sel[...], half, (((0,), (0,)), ((), ())), preferred_element_type=F32
    ).astype(BF16)
    width = out.shape[2]
    nodes = out.shape[0] // 2
    for node in range(nodes):
        for outer in range(2):
            out[slot_of(nodes // 2, node, outer)] = back[
                node * rows : (node + 1) * rows, outer * width : (outer + 1) * width
            ]


def pick_kernel(pick, factor, every, wide):
    width = every.shape[2]
    half = every.shape[0] // 2
    for outer in range(2):
        rows = jnp.concatenate(
            [every[source_of(half, node, outer)] for node in range(half)], axis=0
        )
        part = jnp.dot(pick[...], rows, preferred_element_type=F32)
        wide[:, outer * width : (outer + 1) * width] = (factor[...] * part).astype(BF16)


def shards(nodes, inputs, out_grad, expert_ids, route_probs, gate_w, up_w, down_w):
    gate_w, up_w, down_w = gate_w[0], up_w[0], down_w[0]
    rows, width = inputs.shape
    cape = 2 * rows * expert_ids.shape[1]
    half = nodes // 2
    tokens = nodes * rows
    hidden = down_w.shape[0]
    swap = [(0, 1), (1, 0)]

    (near,) = call(
        "join",
        join_kernel,
        [((2 * rows, width), BF16)],
        inputs, out_grad,
        hbm=(0, 1),
        scratch=[pltpu.SemaphoreType.DMA((2,))],
    )
    far = lax.ppermute(near, "high", swap)
    pick, factor, sel, gate_v, up_v, down_v = call(
        "prep",
        functools.partial(prep_kernel, cape, half, rows),
        [
            ((2 * cape, 2 * tokens), BF16),
            ((2 * cape, 1), F32),
            ((cape, tokens), BF16),
        ]
        + [(w.shape, BF16) for w in (gate_w, up_w, down_w)],
        expert_ids.T, route_probs.T, gate_w, up_w, down_w,
        hbm=range(5),
        scratch=[
            pltpu.VMEM(expert_ids.shape[::-1], jnp.int32),
            pltpu.VMEM(route_probs.shape[::-1], F32),
            pltpu.SemaphoreType.DMA((2,)),
            pltpu.SemaphoreType.DMA((3, 4)),
        ],
        nbytes=6 << 20,
    )
    far, pick = lax.optimization_barrier((far, pick))
    (block,) = call("spread", spread_kernel, [((nodes, 4 * rows, width), BF16)], near, far)
    every = lax.all_to_all(block, GATHER, 0, 0, tiled=True)
    (wide,) = call(
        "pick",
        pick_kernel,
        [((2 * cape, 2 * width), BF16)],
        pick, factor, every,
    )
    across = lax.ppermute(wide, "inner", swap)
    (acc,) = call(
        "third",
        functools.partial(third_kernel, cape),
        [((3, cape, hidden), F32)],
        wide, gate_v, up_v, down_v,
    )
    across, acc = lax.optimization_barrier((across, acc))
    sent, d_gate, d_up = call(
        "hidden",
        functools.partial(hidden_kernel, cape),
        [((cape, 2 * width), BF16), ((cape, hidden), BF16), ((cape, hidden), BF16)],
        across, acc, gate_v, up_v, down_v,
    )
    got = lax.ppermute(sent, "inner", swap)
    (mine,) = call("own", own_kernel, [((cape, 2 * width), F32)], d_gate, d_up, gate_v, up_v)
    (back,) = call(
        "scatter",
        functools.partial(scatter_kernel, rows),
        [((2 * nodes, rows, width), BF16)],
        sel, mine, got,
    )
    home = lax.all_to_all(back, RETURN, 0, 0, tiled=True)
    return jnp.sum(home.astype(F32), axis=0).astype(BF16)


def solution(mesh):
    nodes, locals_ = mesh.shape["node"], mesh.shape["local"]

    def program(inputs, *args):
        width = inputs.shape[1] // locals_
        rows = inputs.shape[0] // nodes
        if locals_ == 4 and width % 128 == 0 and nodes % 4 == 0 and rows & (rows - 1) == 0:
            fine = jax.sharding.Mesh(
                mesh.devices.reshape(2, nodes // 4, 2, 2, 2), ("high", "mid", "low", "outer", "inner")
            )
            node, local = ("high", "mid", "low"), ("outer", "inner")
            body = functools.partial(shards, nodes)
        else:
            fine, node, local = mesh, "node", "local"
            body = functools.partial(general, nodes, locals_)
        placed = (
            P(node, local),
            P(node, local),
            P(),
            P(),
            P(node, None, local),
            P(node, None, local),
            P(node, local, None),
        )
        return jax.shard_map(
            body, mesh=fine, in_specs=placed, out_specs=P(node, local), check_vma=False
        )(inputs, *args)

    return program
```

```python
import functools

import jax
import jax.numpy as jnp
from jax import lax
from jax.experimental import pallas as pl
from jax.experimental.pallas import tpu as pltpu
from jax.sharding import PartitionSpec as P

F32 = jnp.float32
BF16 = jnp.bfloat16
NT = (((1,), (1,)), ((), ()))
RETURN = ("low", "outer", "mid", "high")


def slot_of(half, node, outer):
    return ((((node % 2) * 2 + outer) * (half // 2) + node % half // 2) * 2 + node // half)


GATHER = ("mid", "low", "outer")


def source_of(half, node, outer):
    return (((node // 2) * 2 + node % 2) * 2 + outer)


def slot_tables(expert_ids, route_probs, expert, cape):
    hit = expert_ids == expert
    tokens = expert_ids.shape[0]
    once = jnp.sum(hit.astype(F32), axis=1)
    scale = jnp.sum(jnp.where(hit, route_probs, 0.0), axis=1)
    row = lax.broadcasted_iota(jnp.int32, (tokens, tokens), 0)
    col = lax.broadcasted_iota(jnp.int32, (tokens, tokens), 1)
    rank = jnp.sum(jnp.where(col < row, once[None, :], 0.0), axis=1)
    slots = lax.broadcasted_iota(jnp.int32, (cape, tokens), 0).astype(F32)
    select = jnp.where((rank[None, :] == slots) & (once[None, :] > 0.5), 1.0, 0.0)
    return select, jnp.sum(select * scale[None, :], axis=1)


def partners(size, step):
    if size & (size - 1) == 0:
        return [(i, i ^ step) for i in range(size)]
    return [(i, (i + step) % size) for i in range(size)]


def source(size, me, step):
    if size & (size - 1) == 0:
        return me ^ step
    return lax.rem(me + (size - step), size)


def target(size, me, step):
    if size & (size - 1) == 0:
        return me ^ step
    return lax.rem(me + step, size)


def hidden_terms(gate, up, d_hidden):
    sig = jax.nn.sigmoid(gate)
    d_up = (d_hidden * (gate * sig)).astype(BF16)
    d_gate = (d_hidden * up * sig * (1.0 + gate * (1.0 - sig))).astype(BF16)
    return d_gate, d_up


def general(nodes, locals_, inputs, out_grad, expert_ids, route_probs, gate_w, up_w, down_w):
    expert = lax.axis_index("node")
    me = lax.axis_index("local")
    rows, width = inputs.shape
    cape = 2 * rows * expert_ids.shape[1]
    select, scale = slot_tables(expert_ids, route_probs, expert, cape)
    sel = select.astype(BF16)

    block = jnp.concatenate([inputs, out_grad], axis=0)
    every = lax.all_to_all(
        jnp.broadcast_to(block[None], (nodes,) + block.shape), "node", 0, 0, tiled=True
    )
    s3 = sel.reshape(cape, nodes, 1, rows)
    none = jnp.zeros_like(s3)
    pick = jnp.concatenate(
        [
            jnp.concatenate([s3, none], axis=2).reshape(cape, nodes * 2 * rows),
            jnp.concatenate([none, s3], axis=2).reshape(cape, nodes * 2 * rows),
        ],
        axis=0,
    )
    factor = jnp.concatenate([jnp.ones_like(scale), scale])
    part = jnp.dot(pick, every.reshape(nodes * 2 * rows, width), preferred_element_type=F32)
    part = (factor[:, None] * part).astype(BF16)

    pieces = [part] + [
        lax.ppermute(part, "local", partners(locals_, step)) for step in range(1, locals_)
    ]
    whole = jnp.zeros((2 * cape, width * locals_), BF16)
    for step in range(locals_):
        whole = lax.dynamic_update_slice(
            whole, pieces[step], (0, source(locals_, me, step) * width)
        )
    gate = jnp.dot(whole[:cape], gate_w[0], preferred_element_type=F32)
    up = jnp.dot(whole[:cape], up_w[0], preferred_element_type=F32)
    d_hidden = lax.dot_general(whole[cape:], down_w[0], NT, preferred_element_type=F32)
    d_gate, d_up = hidden_terms(gate, up, d_hidden)
    partial = lax.dot_general(
        d_gate, gate_w[0], NT, preferred_element_type=F32
    ) + lax.dot_general(d_up, up_w[0], NT, preferred_element_type=F32)
    half = partial.astype(BF16)
    total = lax.dynamic_slice_in_dim(partial, me * width, width, 1)
    sent = [
        lax.dynamic_slice_in_dim(half, target(locals_, me, step) * width, width, 1)
        for step in range(1, locals_)
    ]
    for step in range(1, locals_):
        total = total + lax.ppermute(sent[step - 1], "local", partners(locals_, step)).astype(F32)
    d_rows = total.astype(BF16)

    back = lax.dot_general(
        sel, d_rows, (((0,), (0,)), ((), ())), preferred_element_type=F32
    ).astype(BF16)
    mine = lax.all_to_all(back.reshape(nodes, rows, width), "node", 0, 0, tiled=True)
    return jnp.sum(mine.astype(F32), axis=0).astype(BF16)


def column(width, index):
    return pl.ds(pl.multiple_of(index * width, width), width)


def block_terms(piece, cape, at, gate_ref, up_ref, down_ref):
    x, g = piece[:cape, :], piece[cape:, :]
    grad = lax.dot_general(g, down_ref[:, at], NT, preferred_element_type=F32)
    return (
        jnp.dot(x, gate_ref[at, :], preferred_element_type=F32),
        jnp.dot(x, up_ref[at, :], preferred_element_type=F32),
        grad,
    )


def wide_terms(wide, cape, inner, gate_ref, up_ref, down_ref):
    width = wide.shape[1] // 2
    places = [column(width, 2 * outer + inner) for outer in range(2)]
    xs = [wide[:cape, outer * width : (outer + 1) * width] for outer in range(2)]
    gs = [wide[cape:, outer * width : (outer + 1) * width] for outer in range(2)]
    grad = [
        lax.dot_general(g, down_ref[:, at], NT, preferred_element_type=F32)
        for g, at in zip(gs, places)
    ]
    gate = [jnp.dot(x, gate_ref[at, :], preferred_element_type=F32) for x, at in zip(xs, places)]
    up = [jnp.dot(x, up_ref[at, :], preferred_element_type=F32) for x, at in zip(xs, places)]
    return gate[0] + gate[1], up[0] + up[1], grad[0] + grad[1]


def third_kernel(cape, wide, gate_ref, up_ref, down_ref, out):
    terms = wide_terms(wide, cape, lax.axis_index("inner"), gate_ref, up_ref, down_ref)
    for index, term in enumerate(terms):
        out[index] = term


def down_terms(d_gate, d_up, at, gate_ref, up_ref):
    return lax.dot_general(
        d_gate, gate_ref[at, :], NT, preferred_element_type=F32
    ) + lax.dot_general(d_up, up_ref[at, :], NT, preferred_element_type=F32)


def hidden_kernel(cape, wide, acc, gate_ref, up_ref, down_ref, sent, d_gate_ref, d_up_ref):
    width = wide.shape[1] // 2
    inner = lax.axis_index("inner") ^ 1
    terms = wide_terms(wide, cape, inner, gate_ref, up_ref, down_ref)
    gate, up, d_hidden = [acc[index] + term for index, term in enumerate(terms)]
    d_gate, d_up = hidden_terms(gate, up, d_hidden)
    d_gate_ref[...] = d_gate
    d_up_ref[...] = d_up
    for outer in range(2):
        at = column(width, 2 * outer + inner)
        sent[:, outer * width : (outer + 1) * width] = down_terms(
            d_gate, d_up, at, gate_ref, up_ref
        ).astype(BF16)


def own_kernel(d_gate_ref, d_up_ref, gate_ref, up_ref, own):
    width = own.shape[1] // 2
    for outer in range(2):
        at = column(width, 2 * outer + lax.axis_index("inner"))
        own[:, outer * width : (outer + 1) * width] = down_terms(
            d_gate_ref[...], d_up_ref[...], at, gate_ref, up_ref
        )


def call(name, body, outs, *args, hbm=(), scratch=(), limit=4, nbytes=1 << 18):
    args = [
        pltpu.with_memory_space_constraint(arg, pltpu.HBM) if index in hbm else arg
        for index, arg in enumerate(args)
    ]
    vmem = pl.BlockSpec(memory_space=pltpu.VMEM)
    far = pl.BlockSpec(memory_space=pltpu.HBM)
    return pl.pallas_call(
        body,
        out_shape=[jax.ShapeDtypeStruct(shape, dtype) for shape, dtype in outs],
        in_specs=[far if index in hbm else vmem for index in range(len(args))],
        out_specs=[vmem] * len(outs),
        scratch_shapes=list(scratch),
        compiler_params=pltpu.CompilerParams(vmem_limit_bytes=limit << 20),
        cost_estimate=pl.CostEstimate(flops=0, transcendentals=0, bytes_accessed=nbytes),
        name=name,
    )(*args)


def prep_kernel(
    cape, half, rows, ids_hbm, probs_hbm, gate_hbm, up_hbm, down_hbm,
    pick, factor, sel, gate_ref, up_ref, down_ref, ids_ref, probs_ref, sems, weight_sems
):
    pairs = ((ids_hbm, ids_ref), (probs_hbm, probs_ref))
    copies = [
        pltpu.make_async_copy(source_ref, there, sems.at[index])
        for index, (source_ref, there) in enumerate(pairs)
    ]
    parts = weight_sems.shape[1]
    for index, (source_ref, there) in enumerate(
        ((gate_hbm, gate_ref), (up_hbm, up_ref), (down_hbm, down_ref))
    ):
        size = source_ref.shape[0] // parts
        for part in range(parts):
            at = pl.ds(part * size, size)
            copies.append(
                pltpu.make_async_copy(
                    source_ref.at[at, :], there.at[at, :], weight_sems.at[index, part]
                )
            )
    for copy in copies:
        copy.start()
    tokens = ids_ref.shape[1]
    block = 2 * rows
    span = pick.shape[1]

    def grid(height, width, axis):
        return lax.broadcasted_iota(jnp.int32, (height, width), axis)

    def held_of(lane):
        group = lane >> (2 * block).bit_length() - 1
        other = ((lane & block) != 0).astype(jnp.int32) ^ lax.axis_index("high")
        return (other * half + group) * rows + (lane & (rows - 1))

    token = grid(tokens, span, 0)
    held = held_of(grid(tokens, span, 1))
    weight = jnp.concatenate(
        [
            (token < held).astype(BF16),
            (token == held).astype(BF16),
            (grid(tokens, tokens, 0) < grid(tokens, tokens, 1)).astype(BF16),
        ],
        axis=1,
    )
    slot = grid(2 * cape, span, 0)
    side = (grid(2 * cape, span, 1) & rows) != 0
    wanted = jnp.where(side, slot - cape, slot).astype(F32)

    copies[0].wait()
    expert = lax.axis_index("high") * half + 2 * lax.axis_index("mid") + lax.axis_index("low")
    hit = ids_ref[...] == expert
    once = jnp.sum(jnp.where(hit, 1.0, 0.0), axis=0, keepdims=True)
    wide = jnp.broadcast_to(once, (8, tokens)).astype(BF16)
    counts = jnp.dot(wide, weight, preferred_element_type=F32)
    there = jnp.where(counts[:1, span : 2 * span] > 0.5, counts[:1, :span], -2.0 * cape)
    pick[...] = jnp.where(there == wanted, 1.0, 0.0).astype(BF16)
    code = jnp.where(once > 0.5, counts[:1, 2 * span :], -2.0 * cape)
    mine = code == grid(cape, tokens, 0).astype(F32)
    sel[...] = jnp.where(mine, 1.0, 0.0).T.astype(BF16)
    copies[1].wait()
    scale = jnp.sum(jnp.where(hit, probs_ref[...], 0.0), axis=0, keepdims=True)
    factor[:cape, :] = jnp.ones((cape, 1), F32)
    factor[cape:, :] = jnp.sum(jnp.where(mine, scale, 0.0), axis=1, keepdims=True)
    for copy in copies[2:]:
        copy.wait()


def join_kernel(x_hbm, g_hbm, out, sems):
    rows = x_hbm.shape[0]
    copies = [
        pltpu.make_async_copy(x_hbm, out.at[pl.ds(0, rows), :], sems.at[0]),
        pltpu.make_async_copy(g_hbm, out.at[pl.ds(rows, rows), :], sems.at[1]),
    ]
    for copy in copies:
        copy.start()
    for copy in copies:
        copy.wait()


def spread_kernel(near, far, out):
    rows = near.shape[0]
    for index in range(out.shape[0]):
        out[index, :rows, :] = near[...]
        out[index, rows:, :] = far[...]


def scatter_kernel(rows, sel, mine, got, out):
    half = (mine[...] + got[...].astype(F32)).astype(BF16)
    back = jnp.dot(sel[...], half, preferred_element_type=F32).astype(BF16)
    width = out.shape[2]
    nodes = out.shape[0] // 2
    for node in range(nodes):
        for outer in range(2):
            out[slot_of(nodes // 2, node, outer)] = back[
                node * rows : (node + 1) * rows, outer * width : (outer + 1) * width
            ]


def pick_kernel(pick, factor, every, wide):
    width = every.shape[2]
    half = every.shape[0] // 2
    for outer in range(2):
        rows = jnp.concatenate(
            [every[source_of(half, node, outer)] for node in range(half)], axis=0
        )
        part = jnp.dot(pick[...], rows, preferred_element_type=F32)
        wide[:, outer * width : (outer + 1) * width] = (factor[...] * part).astype(BF16)


def shards(nodes, inputs, out_grad, expert_ids, route_probs, gate_w, up_w, down_w):
    gate_w, up_w, down_w = gate_w[0], up_w[0], down_w[0]
    rows, width = inputs.shape
    cape = 2 * rows * expert_ids.shape[1]
    half = nodes // 2
    tokens = nodes * rows
    hidden = down_w.shape[0]
    swap = [(0, 1), (1, 0)]

    (near,) = call(
        "join",
        join_kernel,
        [((2 * rows, width), BF16)],
        inputs, out_grad,
        hbm=(0, 1),
        scratch=[pltpu.SemaphoreType.DMA((2,))],
    )
    far = lax.ppermute(near, "high", swap)
    pick, factor, sel, gate_v, up_v, down_v = call(
        "prep",
        functools.partial(prep_kernel, cape, half, rows),
        [
            ((2 * cape, 2 * tokens), BF16),
            ((2 * cape, 1), F32),
            ((tokens, cape), BF16),
        ]
        + [(w.shape, BF16) for w in (gate_w, up_w, down_w)],
        expert_ids.T, route_probs.T, gate_w, up_w, down_w,
        hbm=range(5),
        scratch=[
            pltpu.VMEM(expert_ids.shape[::-1], jnp.int32),
            pltpu.VMEM(route_probs.shape[::-1], F32),
            pltpu.SemaphoreType.DMA((2,)),
            pltpu.SemaphoreType.DMA((3, 4)),
        ],
        nbytes=6 << 20,
    )
    far, pick = lax.optimization_barrier((far, pick))
    (block,) = call("spread", spread_kernel, [((nodes, 4 * rows, width), BF16)], near, far)
    every = lax.all_to_all(block, GATHER, 0, 0, tiled=True)
    (wide,) = call(
        "pick",
        pick_kernel,
        [((2 * cape, 2 * width), BF16)],
        pick, factor, every,
    )
    across = lax.ppermute(wide, "inner", swap)
    (acc,) = call(
        "third",
        functools.partial(third_kernel, cape),
        [((3, cape, hidden), F32)],
        wide, gate_v, up_v, down_v,
    )
    across, acc = lax.optimization_barrier((across, acc))
    sent, d_gate, d_up = call(
        "hidden",
        functools.partial(hidden_kernel, cape),
        [((cape, 2 * width), BF16), ((cape, hidden), BF16), ((cape, hidden), BF16)],
        across, acc, gate_v, up_v, down_v,
    )
    got = lax.ppermute(sent, "inner", swap)
    (mine,) = call("own", own_kernel, [((cape, 2 * width), F32)], d_gate, d_up, gate_v, up_v)
    (back,) = call(
        "scatter",
        functools.partial(scatter_kernel, rows),
        [((2 * nodes, rows, width), BF16)],
        sel, mine, got,
    )
    home = lax.all_to_all(back, RETURN, 0, 0, tiled=True)
    return jnp.sum(home.astype(F32), axis=0).astype(BF16)


def solution(mesh):
    nodes, locals_ = mesh.shape["node"], mesh.shape["local"]

    def program(inputs, *args):
        width = inputs.shape[1] // locals_
        rows = inputs.shape[0] // nodes
        if locals_ == 4 and width % 128 == 0 and nodes % 4 == 0 and rows & (rows - 1) == 0:
            fine = jax.sharding.Mesh(
                mesh.devices.reshape(2, nodes // 4, 2, 2, 2), ("high", "mid", "low", "outer", "inner")
            )
            node, local = ("high", "mid", "low"), ("outer", "inner")
            body = functools.partial(shards, nodes)
        else:
            fine, node, local = mesh, "node", "local"
            body = functools.partial(general, nodes, locals_)
        placed = (
            P(node, local),
            P(node, local),
            P(),
            P(),
            P(node, None, local),
            P(node, None, local),
            P(node, local, None),
        )
        return jax.shard_map(
            body, mesh=fine, in_specs=placed, out_specs=P(node, local), check_vma=False
        )(inputs, *args)

    return program
```

```python
import functools

import jax
import jax.numpy as jnp
from jax import lax
from jax.experimental import pallas as pl
from jax.experimental.pallas import tpu as pltpu
from jax.sharding import PartitionSpec as P

F32 = jnp.float32
BF16 = jnp.bfloat16
NT = (((1,), (1,)), ((), ()))
RETURN = ("low", "outer", "mid", "high")


def slot_of(half, node, outer):
    return ((((node % 2) * 2 + outer) * (half // 2) + node % half // 2) * 2 + node // half)


GATHER = ("mid", "low", "outer")


def source_of(half, node, outer):
    return (((node // 2) * 2 + node % 2) * 2 + outer)


def slot_tables(expert_ids, route_probs, expert, cape):
    hit = expert_ids == expert
    tokens = expert_ids.shape[0]
    once = jnp.sum(hit.astype(F32), axis=1)
    scale = jnp.sum(jnp.where(hit, route_probs, 0.0), axis=1)
    row = lax.broadcasted_iota(jnp.int32, (tokens, tokens), 0)
    col = lax.broadcasted_iota(jnp.int32, (tokens, tokens), 1)
    rank = jnp.sum(jnp.where(col < row, once[None, :], 0.0), axis=1)
    slots = lax.broadcasted_iota(jnp.int32, (cape, tokens), 0).astype(F32)
    select = jnp.where((rank[None, :] == slots) & (once[None, :] > 0.5), 1.0, 0.0)
    return select, jnp.sum(select * scale[None, :], axis=1)


def partners(size, step):
    if size & (size - 1) == 0:
        return [(i, i ^ step) for i in range(size)]
    return [(i, (i + step) % size) for i in range(size)]


def source(size, me, step):
    if size & (size - 1) == 0:
        return me ^ step
    return lax.rem(me + (size - step), size)


def target(size, me, step):
    if size & (size - 1) == 0:
        return me ^ step
    return lax.rem(me + step, size)


def hidden_terms(gate, up, d_hidden):
    sig = jax.nn.sigmoid(gate)
    d_up = (d_hidden * (gate * sig)).astype(BF16)
    d_gate = (d_hidden * up * sig * (1.0 + gate * (1.0 - sig))).astype(BF16)
    return d_gate, d_up


def general(nodes, locals_, inputs, out_grad, expert_ids, route_probs, gate_w, up_w, down_w):
    expert = lax.axis_index("node")
    me = lax.axis_index("local")
    rows, width = inputs.shape
    cape = 2 * rows * expert_ids.shape[1]
    select, scale = slot_tables(expert_ids, route_probs, expert, cape)
    sel = select.astype(BF16)

    block = jnp.concatenate([inputs, out_grad], axis=0)
    every = lax.all_to_all(
        jnp.broadcast_to(block[None], (nodes,) + block.shape), "node", 0, 0, tiled=True
    )
    s3 = sel.reshape(cape, nodes, 1, rows)
    none = jnp.zeros_like(s3)
    pick = jnp.concatenate(
        [
            jnp.concatenate([s3, none], axis=2).reshape(cape, nodes * 2 * rows),
            jnp.concatenate([none, s3], axis=2).reshape(cape, nodes * 2 * rows),
        ],
        axis=0,
    )
    factor = jnp.concatenate([jnp.ones_like(scale), scale])
    part = jnp.dot(pick, every.reshape(nodes * 2 * rows, width), preferred_element_type=F32)
    part = (factor[:, None] * part).astype(BF16)

    pieces = [part] + [
        lax.ppermute(part, "local", partners(locals_, step)) for step in range(1, locals_)
    ]
    whole = jnp.zeros((2 * cape, width * locals_), BF16)
    for step in range(locals_):
        whole = lax.dynamic_update_slice(
            whole, pieces[step], (0, source(locals_, me, step) * width)
        )
    gate = jnp.dot(whole[:cape], gate_w[0], preferred_element_type=F32)
    up = jnp.dot(whole[:cape], up_w[0], preferred_element_type=F32)
    d_hidden = lax.dot_general(whole[cape:], down_w[0], NT, preferred_element_type=F32)
    d_gate, d_up = hidden_terms(gate, up, d_hidden)
    partial = lax.dot_general(
        d_gate, gate_w[0], NT, preferred_element_type=F32
    ) + lax.dot_general(d_up, up_w[0], NT, preferred_element_type=F32)
    half = partial.astype(BF16)
    total = lax.dynamic_slice_in_dim(partial, me * width, width, 1)
    sent = [
        lax.dynamic_slice_in_dim(half, target(locals_, me, step) * width, width, 1)
        for step in range(1, locals_)
    ]
    for step in range(1, locals_):
        total = total + lax.ppermute(sent[step - 1], "local", partners(locals_, step)).astype(F32)
    d_rows = total.astype(BF16)

    back = lax.dot_general(
        sel, d_rows, (((0,), (0,)), ((), ())), preferred_element_type=F32
    ).astype(BF16)
    mine = lax.all_to_all(back.reshape(nodes, rows, width), "node", 0, 0, tiled=True)
    return jnp.sum(mine.astype(F32), axis=0).astype(BF16)


def column(width, index):
    return pl.ds(pl.multiple_of(index * width, width), width)


def block_terms(piece, cape, at, gate_ref, up_ref, down_ref):
    x, g = piece[:cape, :], piece[cape:, :]
    grad = lax.dot_general(g, down_ref[:, at], NT, preferred_element_type=F32)
    return (
        jnp.dot(x, gate_ref[at, :], preferred_element_type=F32),
        jnp.dot(x, up_ref[at, :], preferred_element_type=F32),
        grad,
    )


def wide_terms(wide, cape, inner, gate_ref, up_ref, down_ref):
    width = wide.shape[1] // 2
    places = [column(width, 2 * outer + inner) for outer in range(2)]
    xs = [wide[:cape, outer * width : (outer + 1) * width] for outer in range(2)]
    gs = [wide[cape:, outer * width : (outer + 1) * width] for outer in range(2)]
    grad = [
        lax.dot_general(g, down_ref[:, at], NT, preferred_element_type=F32)
        for g, at in zip(gs, places)
    ]
    gate = [jnp.dot(x, gate_ref[at, :], preferred_element_type=F32) for x, at in zip(xs, places)]
    up = [jnp.dot(x, up_ref[at, :], preferred_element_type=F32) for x, at in zip(xs, places)]
    return gate[0] + gate[1], up[0] + up[1], grad[0] + grad[1]


def third_kernel(cape, wide, gate_ref, up_ref, down_ref, out):
    terms = wide_terms(wide, cape, lax.axis_index("inner"), gate_ref, up_ref, down_ref)
    for index, term in enumerate(terms):
        out[index] = term


def down_terms(d_gate, d_up, at, gate_ref, up_ref):
    return lax.dot_general(
        d_gate, gate_ref[at, :], NT, preferred_element_type=F32
    ) + lax.dot_general(d_up, up_ref[at, :], NT, preferred_element_type=F32)


def hidden_kernel(cape, wide, acc, gate_ref, up_ref, down_ref, sent, d_gate_ref, d_up_ref):
    width = wide.shape[1] // 2
    inner = lax.axis_index("inner") ^ 1
    terms = wide_terms(wide, cape, inner, gate_ref, up_ref, down_ref)
    gate, up, d_hidden = [acc[index] + term for index, term in enumerate(terms)]
    d_gate, d_up = hidden_terms(gate, up, d_hidden)
    d_gate_ref[...] = d_gate
    d_up_ref[...] = d_up
    for outer in range(2):
        at = column(width, 2 * outer + inner)
        sent[:, outer * width : (outer + 1) * width] = down_terms(
            d_gate, d_up, at, gate_ref, up_ref
        ).astype(BF16)


def own_kernel(d_gate_ref, d_up_ref, gate_ref, up_ref, own):
    width = own.shape[1] // 2
    for outer in range(2):
        at = column(width, 2 * outer + lax.axis_index("inner"))
        own[:, outer * width : (outer + 1) * width] = down_terms(
            d_gate_ref[...], d_up_ref[...], at, gate_ref, up_ref
        )


def call(name, body, outs, *args, hbm=(), scratch=(), limit=4, nbytes=1 << 18, flags=None):
    args = [
        pltpu.with_memory_space_constraint(arg, pltpu.HBM) if index in hbm else arg
        for index, arg in enumerate(args)
    ]
    vmem = pl.BlockSpec(memory_space=pltpu.VMEM)
    far = pl.BlockSpec(memory_space=pltpu.HBM)
    return pl.pallas_call(
        body,
        out_shape=[jax.ShapeDtypeStruct(shape, dtype) for shape, dtype in outs],
        in_specs=[far if index in hbm else vmem for index in range(len(args))],
        out_specs=[vmem] * len(outs),
        scratch_shapes=list(scratch),
        compiler_params=pltpu.CompilerParams(vmem_limit_bytes=limit << 20, flags=flags),
        cost_estimate=pl.CostEstimate(flops=0, transcendentals=0, bytes_accessed=nbytes),
        name=name,
    )(*args)


def prep_kernel(
    cape, half, rows, ids_hbm, probs_hbm, gate_hbm, up_hbm, down_hbm,
    pick, factor, sel, gate_ref, up_ref, down_ref, ids_ref, probs_ref, sems, weight_sems
):
    pairs = ((ids_hbm, ids_ref), (probs_hbm, probs_ref))
    copies = [
        pltpu.make_async_copy(source_ref, there, sems.at[index])
        for index, (source_ref, there) in enumerate(pairs)
    ]
    parts = weight_sems.shape[1]
    for index, (source_ref, there) in enumerate(
        ((gate_hbm, gate_ref), (up_hbm, up_ref), (down_hbm, down_ref))
    ):
        size = source_ref.shape[0] // parts
        for part in range(parts):
            at = pl.ds(part * size, size)
            copies.append(
                pltpu.make_async_copy(
                    source_ref.at[at, :], there.at[at, :], weight_sems.at[index, part]
                )
            )
    for copy in copies:
        copy.start()
    tokens = ids_ref.shape[1]
    block = 2 * rows
    span = pick.shape[1]

    def grid(height, width, axis):
        return lax.broadcasted_iota(jnp.int32, (height, width), axis)

    def held_of(lane):
        group = lane >> (2 * block).bit_length() - 1
        other = ((lane & block) != 0).astype(jnp.int32) ^ lax.axis_index("high")
        return (other * half + group) * rows + (lane & (rows - 1))

    token = grid(tokens, span, 0)
    held = held_of(grid(tokens, span, 1))
    weight = jnp.concatenate(
        [
            (token < held).astype(BF16),
            (token == held).astype(BF16),
            (grid(tokens, tokens, 0) < grid(tokens, tokens, 1)).astype(BF16),
        ],
        axis=1,
    )
    slot = grid(2 * cape, span, 0)
    side = (grid(2 * cape, span, 1) & rows) != 0
    wanted = jnp.where(side, slot - cape, slot).astype(F32)

    copies[0].wait()
    expert = lax.axis_index("high") * half + 2 * lax.axis_index("mid") + lax.axis_index("low")
    hit = ids_ref[...] == expert
    once = jnp.sum(jnp.where(hit, 1.0, 0.0), axis=0, keepdims=True)
    wide = jnp.broadcast_to(once, (8, tokens)).astype(BF16)
    counts = jnp.dot(wide, weight, preferred_element_type=F32)
    there = jnp.where(counts[:1, span : 2 * span] > 0.5, counts[:1, :span], -2.0 * cape)
    pick[...] = jnp.where(there == wanted, 1.0, 0.0).astype(BF16)
    code = jnp.where(once > 0.5, counts[:1, 2 * span :], -2.0 * cape)
    mine = code == grid(cape, tokens, 0).astype(F32)
    sel[...] = jnp.where(mine, 1.0, 0.0).T.astype(BF16)
    copies[1].wait()
    scale = jnp.sum(jnp.where(hit, probs_ref[...], 0.0), axis=0, keepdims=True)
    factor[:cape, :] = jnp.ones((cape, 1), F32)
    factor[cape:, :] = jnp.sum(jnp.where(mine, scale, 0.0), axis=1, keepdims=True)
    for copy in copies[2:]:
        copy.wait()


def join_kernel(x_hbm, g_hbm, out, sems):
    rows = x_hbm.shape[0]
    copies = [
        pltpu.make_async_copy(x_hbm, out.at[pl.ds(0, rows), :], sems.at[0]),
        pltpu.make_async_copy(g_hbm, out.at[pl.ds(rows, rows), :], sems.at[1]),
    ]
    for copy in copies:
        copy.start()
    for copy in copies:
        copy.wait()


def spread_kernel(near, far, out):
    rows = near.shape[0]
    for index in range(out.shape[0]):
        out[index, :rows, :] = near[...]
        out[index, rows:, :] = far[...]


def scatter_kernel(rows, sel, mine, got, out):
    half = (mine[...] + got[...].astype(F32)).astype(BF16)
    back = jnp.dot(sel[...], half, preferred_element_type=F32).astype(BF16)
    width = out.shape[2]
    nodes = out.shape[0] // 2
    for node in range(nodes):
        for outer in range(2):
            out[slot_of(nodes // 2, node, outer)] = back[
                node * rows : (node + 1) * rows, outer * width : (outer + 1) * width
            ]


def pick_kernel(pick, factor, every, wide):
    width = every.shape[2]
    half = every.shape[0] // 2
    for outer in range(2):
        rows = jnp.concatenate(
            [every[source_of(half, node, outer)] for node in range(half)], axis=0
        )
        part = jnp.dot(pick[...], rows, preferred_element_type=F32)
        wide[:, outer * width : (outer + 1) * width] = (factor[...] * part).astype(BF16)


def shards(nodes, inputs, out_grad, expert_ids, route_probs, gate_w, up_w, down_w):
    gate_w, up_w, down_w = gate_w[0], up_w[0], down_w[0]
    rows, width = inputs.shape
    cape = 2 * rows * expert_ids.shape[1]
    half = nodes // 2
    tokens = nodes * rows
    hidden = down_w.shape[0]
    swap = [(0, 1), (1, 0)]

    (near,) = call(
        "join",
        join_kernel,
        [((2 * rows, width), BF16)],
        inputs, out_grad,
        hbm=(0, 1),
        scratch=[pltpu.SemaphoreType.DMA((2,))],
    )
    far = lax.ppermute(near, "high", swap)
    pick, factor, sel, gate_v, up_v, down_v = call(
        "prep",
        functools.partial(prep_kernel, cape, half, rows),
        [
            ((2 * cape, 2 * tokens), BF16),
            ((2 * cape, 1), F32),
            ((tokens, cape), BF16),
        ]
        + [(w.shape, BF16) for w in (gate_w, up_w, down_w)],
        expert_ids.T, route_probs.T, gate_w, up_w, down_w,
        hbm=range(5),
        scratch=[
            pltpu.VMEM(expert_ids.shape[::-1], jnp.int32),
            pltpu.VMEM(route_probs.shape[::-1], F32),
            pltpu.SemaphoreType.DMA((2,)),
            pltpu.SemaphoreType.DMA((3, 4)),
        ],
        nbytes=6 << 20,
    )
    far, pick = lax.optimization_barrier((far, pick))
    (block,) = call("spread", spread_kernel, [((nodes, 4 * rows, width), BF16)], near, far)
    every = lax.all_to_all(block, GATHER, 0, 0, tiled=True)
    (wide,) = call(
        "pick",
        pick_kernel,
        [((2 * cape, 2 * width), BF16)],
        pick, factor, every,
    )
    across = lax.ppermute(wide, "inner", swap)
    (acc,) = call(
        "third",
        functools.partial(third_kernel, cape),
        [((3, cape, hidden), F32)],
        wide, gate_v, up_v, down_v,
    )
    across, acc = lax.optimization_barrier((across, acc))
    sent, d_gate, d_up = call(
        "hidden",
        functools.partial(hidden_kernel, cape),
        [((cape, 2 * width), BF16), ((cape, hidden), BF16), ((cape, hidden), BF16)],
        across, acc, gate_v, up_v, down_v,
    )
    got = lax.ppermute(sent, "inner", swap)
    (mine,) = call("own", own_kernel, [((cape, 2 * width), F32)], d_gate, d_up, gate_v, up_v)
    (back,) = call(
        "scatter",
        functools.partial(scatter_kernel, rows),
        [((2 * nodes, rows, width), BF16)],
        sel, mine, got,
    )
    home = lax.all_to_all(back, RETURN, 0, 0, tiled=True)
    return jnp.sum(home.astype(F32), axis=0).astype(BF16)


def solution(mesh):
    nodes, locals_ = mesh.shape["node"], mesh.shape["local"]

    def program(inputs, *args):
        width = inputs.shape[1] // locals_
        rows = inputs.shape[0] // nodes
        if locals_ == 4 and width % 128 == 0 and nodes % 4 == 0 and rows & (rows - 1) == 0:
            fine = jax.sharding.Mesh(
                mesh.devices.reshape(2, nodes // 4, 2, 2, 2), ("high", "mid", "low", "outer", "inner")
            )
            node, local = ("high", "mid", "low"), ("outer", "inner")
            body = functools.partial(shards, nodes)
        else:
            fine, node, local = mesh, "node", "local"
            body = functools.partial(general, nodes, locals_)
        placed = (
            P(node, local),
            P(node, local),
            P(),
            P(),
            P(node, None, local),
            P(node, None, local),
            P(node, local, None),
        )
        return jax.shard_map(
            body, mesh=fine, in_specs=placed, out_specs=P(node, local), check_vma=False
        )(inputs, *args)

    return program
```
